512 devices in a mesh: dp: 32 (over y, x), seq: 16 (over z, core).
Axes of the slice: x: 4, y: 8, z: 8, core: 2. Of those that a mesh axis runs over, the one named last changes fastest.
Arguments:
- grad_out: bfloat16 [65536, 1280], P(('dp', 'seq')), may hold values from -6 to 6
- saved_input: bfloat16 [65536, 1280], P(('dp', 'seq')), may hold values from -6 to 6
- pre_glu: bfloat16 [65536, 2560], P(('dp', 'seq')), may hold values from -6 to 6
- queries: bfloat16 [65536, 1280], P('dp', 'seq'), may hold values from -8 to 8
- keys: bfloat16 [65536, 1280], P('dp', 'seq'), may hold values from -8 to 8
- values: bfloat16 [65536, 1280], P('dp', 'seq'), may hold values from -6 to 6
- frame_counts: int32 [32, 8], P('dp'), may hold values from 1 to 1024, 2048 in all within a row
- norm_gain: float32 [1280], replicated, may hold values from 0.5 to 1.5
- kernel: float32 [31, 1280], replicated, may hold values from -1 to 1
- w_in: bfloat16 [1280, 2560], P('dp'), may hold values from -0.15625 to 0.15625
- w_conv_out: bfloat16 [1280, 1280], P('dp'), may hold values from -0.15625 to 0.15625
- w_attn_out: bfloat16 [1280, 1280], P('dp'), may hold values from -0.15625 to 0.15625
Outputs:
- resid_grad: bfloat16 [65536, 1280], P(('dp', 'seq'))
- query_grad: bfloat16 [65536, 1280], P('dp', 'seq')
- key_grad: bfloat16 [65536, 1280], P('dp', 'seq')
- value_grad: bfloat16 [65536, 1280], P('dp', 'seq')
- kernel_grad: float32 [31, 1280], replicated
- gain_grad: float32 [1280], replicated
The draws below stay inside these ranges and needn't reach their ends.
Inputs may be any that keep to these rules, and one draw needn't show every extreme that they name: `frame_counts`: each row sums to 2048; its largest entry is exactly 1024.
All inputs are finite; a program needn't handle non-finite values.
Results may differ from the reference program's by a relative error of at most 0.018.
Values may be sent and summed in bfloat16 or wider, within the bound.
No kernel may reach another device: no remote copies, remote signals or barrier semaphores. Data moves between devices by JAX's collectives and lax.ppermute only.
A program may use at most 64 MiB of HBM per device.

```python
import math
import jax
import jax.numpy as jnp
import numpy as np
from jax import lax

D = 1280
H = 16
HD = 80
KW = 31
UTTS = 8
TOTAL = 2048
FRAMES = 65536
MOST = 1024
N_DP = 32


def drawn_pair(key):
    base = jax.random.fold_in(key, 11)
    query_key, other_key = jax.random.split(base, 2)
    query = jnp.clip(jax.random.normal(query_key, (FRAMES, D), jnp.float32), -6.0, 6.0)
    keyset = jnp.clip(jax.random.normal(other_key, (FRAMES, D), jnp.float32), -6.0, 6.0)
    return (query, keyset)


def draw_queries(key, part):
    return drawn_pair(key)[0].astype(jnp.bfloat16)


def draw_keys(key, part):
    return drawn_pair(key)[1].astype(jnp.bfloat16)


def levels(key, shape, cuts, smallest, high):
    level = 1.0
    for dim, parts in cuts:
        steps = jax.random.uniform(jax.random.fold_in(jax.random.fold_in(key, 6), dim), (parts,), jnp.float32, smallest / len(cuts), high / len(cuts))
        level = level * jnp.repeat(jnp.exp(steps), shape[dim] // parts).reshape((-1,) + (1,) * (len(shape) - 1 - dim))
    return level


def profile(count, total, reach, lean):
    portions = [(1 << 20) // math.isqrt(rank ** lean) + 1 for rank in range(2, count + 1)]
    spare, holding = total - reach - (count - 1), [1] * (count - 1)
    while spare > 0:
        free = [i for i in range(count - 1) if holding[i] < reach]
        mass, budget = sum([portions[i] for i in free]), spare
        for i in free:
            more = min(reach - holding[i], max(1, budget * portions[i] // mass), spare)
            holding[i] = holding[i] + more
            spare = spare - more
    return np.array([reach] + holding)


def uneven(key, number_of, total, bound, lean):
    if number_of == 2:
        one = jax.random.randint(key, (), max(1, total - bound), min(bound, total - 1) + 1)
        return jnp.stack([one, total - one])
    lengths = jnp.asarray(profile(number_of, total, bound, lean), jnp.int32)
    couples = (number_of - 1) // 2
    source_of, receiver = lengths[1:1 + 2 * couples:2], lengths[2:2 + 2 * couples:2]
    margin = jnp.minimum(source_of - 1, bound - receiver)
    shifted = jax.random.randint(jax.random.fold_in(key, 1), (couples,), 0, 1 << 20) % (margin + 1)
    lengths = lengths.at[1:1 + 2 * couples:2].set(source_of - shifted).at[2:2 + 2 * couples:2].set(receiver + shifted)
    return lengths[jax.random.permutation(jax.random.fold_in(key, 2), number_of)]


def scatter_about(own_key, shape, scale, most, cuts=(), kind=jnp.bfloat16):
    level = levels(own_key, shape, cuts, -0.22, 0.18) if cuts else 1.0
    result = jax.random.normal(own_key, shape, jnp.float32) * scale * level
    return jnp.minimum(jnp.maximum(result, -most), most).astype(kind)


def setup_inputs(seed: int = 0) -> dict:
    splits = jax.random.split(jax.random.key(seed), 13)
    grad_out = scatter_about(splits[0], (FRAMES, D), 1.0, 6.0, ((0, 512),))
    saved_input = scatter_about(splits[1], (FRAMES, D), 1.0, 6.0, ((0, 512),))
    pre_glu = scatter_about(splits[2], (FRAMES, 2 * D), 1.0, 6.0, ((0, 512),))
    queries = draw_queries(jax.random.fold_in(splits[12], 71), 0)
    keys = draw_keys(jax.random.fold_in(splits[12], 71), 0)
    values = scatter_about(splits[5], (FRAMES, D), 1.0, 6.0, ((0, 32), (1, 16)))
    frame_counts = jax.vmap(lambda own: uneven(own, UTTS, TOTAL, MOST, 2))(jax.random.split(splits[6], N_DP)).reshape((N_DP, UTTS)).astype(jnp.int32)
    norm_gain = jnp.clip(1.0 + 0.1 * jax.random.normal(splits[7], (D,), jnp.float32), 0.5, 1.5)
    kernel = scatter_about(splits[8], (KW, D), KW ** -0.5, 1.0, (), jnp.float32)
    w_in = scatter_about(splits[9], (D, 2 * D), D ** -0.5, 0.15625, ((0, 32),))
    w_conv_out = scatter_about(splits[10], (D, D), D ** -0.5, 0.15625, ((0, 32),))
    w_attn_out = scatter_about(splits[11], (D, D), D ** -0.5, 0.15625, ((0, 32),))
    return dict(grad_out=grad_out, saved_input=saved_input, pre_glu=pre_glu, queries=queries, keys=keys, values=values, frame_counts=frame_counts, norm_gain=norm_gain, kernel=kernel, w_in=w_in, w_conv_out=w_conv_out, w_attn_out=w_attn_out)


def segments_of(frame_lens, positions):
    ends = jnp.cumsum(frame_lens).astype(jnp.int32)
    counted = lax.optimization_barrier(jnp.sum((positions[:, None] >= ends[None, :]).astype(jnp.int32), axis=1)).astype(jnp.int32)
    return jnp.where(positions < 0, jnp.int32(-1), counted).astype(jnp.int32)

def group_conv(grad_rows, input_rows, pre_rows, frame_lens, norm_gain, kernel, w_in, w_conv_out, w_attn_out):
    half = KW // 2
    length = grad_rows.shape[0]
    seg_own = segments_of(frame_lens, jnp.arange(length, dtype=jnp.int32))
    seg_pad = segments_of(frame_lens, jnp.arange(-half, length + half, dtype=jnp.int32))
    first_half = pre_rows[:, :D].astype(jnp.float32)
    gate_sig = jax.nn.sigmoid(pre_rows[:, D:].astype(jnp.float32))
    glu_out = (first_half * gate_sig).astype(jnp.bfloat16)
    glu_pad = jnp.pad(glu_out.astype(jnp.float32), ((half, half), (0, 0)))
    conv_out = jnp.zeros((length, D), jnp.float32)
    for tap_index in range(KW):
        match = (seg_pad[tap_index:tap_index + length] == seg_own).astype(jnp.float32)[:, None]
        conv_out = conv_out + kernel[tap_index] * glu_pad[tap_index:tap_index + length] * match
    conv_out_grad = jnp.dot(grad_rows, w_conv_out.T, preferred_element_type=jnp.float32)
    conv_sig = jax.nn.sigmoid(conv_out)
    conv_grad = (conv_out_grad * conv_sig * (1.0 + conv_out * (1.0 - conv_sig))).astype(jnp.bfloat16)
    grad_float = conv_grad.astype(jnp.float32)
    grad_pad = jnp.pad(grad_float, ((half, half), (0, 0)))
    glu_grad = jnp.zeros((length, D), jnp.float32)
    kernel_rows = []
    for tap_index in range(KW):
        back = 2 * half - tap_index
        match_back = (seg_pad[back:back + length] == seg_own).astype(jnp.float32)[:, None]
        glu_grad = glu_grad + kernel[tap_index] * grad_pad[back:back + length] * match_back
        match = (seg_pad[tap_index:tap_index + length] == seg_own).astype(jnp.float32)[:, None]
        kernel_rows.append(lax.optimization_barrier(jnp.sum(grad_float * glu_pad[tap_index:tap_index + length] * match, axis=0)))
    glu_in_grad = jnp.concatenate([glu_grad * gate_sig, glu_grad * first_half * gate_sig * (1.0 - gate_sig)], axis=1).astype(jnp.bfloat16)
    norm_grad = jnp.dot(glu_in_grad, w_in.T, preferred_element_type=jnp.float32)
    inputs = input_rows.astype(jnp.float32)
    centred = inputs - lax.optimization_barrier(jnp.mean(inputs, axis=1, keepdims=True))
    inv_std = 1.0 / jnp.sqrt(lax.optimization_barrier(jnp.mean(centred * centred, axis=1, keepdims=True)) + 1e-05)
    normed = centred * inv_std
    scaled_grad = norm_grad * norm_gain
    input_grad = inv_std * (scaled_grad - lax.optimization_barrier(jnp.mean(scaled_grad, axis=1, keepdims=True)) - normed * lax.optimization_barrier(jnp.mean(scaled_grad * normed, axis=1, keepdims=True)))
    resid_grad = (grad_rows.astype(jnp.float32) + input_grad).astype(jnp.bfloat16)
    gain_term = lax.optimization_barrier(jnp.sum(norm_grad * normed, axis=0))
    ctx_grad = jnp.dot(resid_grad, w_attn_out.T, preferred_element_type=jnp.float32).astype(jnp.bfloat16)
    return (resid_grad, ctx_grad, jnp.stack(kernel_rows), gain_term, seg_own)

def head_backward(query_head, key_head, value_head, out_grad, seg_own):
    scale = 1.0 / math.sqrt(HD)
    scores = jnp.dot(query_head, key_head.T, preferred_element_type=jnp.float32) * scale
    scores = jnp.where(seg_own[:, None] == seg_own[None, :], scores, -1e+30)
    peak = lax.optimization_barrier(jnp.max(scores, axis=1, keepdims=True))
    expd = jnp.exp(scores - peak)
    probs = expd / lax.optimization_barrier(jnp.sum(expd, axis=1, keepdims=True))
    probs_low = probs.astype(jnp.bfloat16)
    value_grad = jnp.dot(probs_low.T, out_grad, preferred_element_type=jnp.float32).astype(jnp.bfloat16)
    prob_grad = jnp.dot(out_grad, value_head.T, preferred_element_type=jnp.float32)
    delta = lax.optimization_barrier(jnp.sum(probs * prob_grad, axis=1, keepdims=True))
    score_grad = (probs * (prob_grad - delta)).astype(jnp.bfloat16)
    query_grad = (jnp.dot(score_grad, key_head, preferred_element_type=jnp.float32) * scale).astype(jnp.bfloat16)
    key_grad = (jnp.dot(score_grad.T, query_head, preferred_element_type=jnp.float32) * scale).astype(jnp.bfloat16)
    return (query_grad, key_grad, value_grad)

def reference(grad_out, saved_input, pre_glu, queries, keys, values, frame_counts, norm_gain, kernel, w_in, w_conv_out, w_attn_out):

    def split_heads(array):
        return array.reshape(TOTAL, H, HD).transpose(1, 0, 2)

    def join_heads(array):
        return array.transpose(1, 0, 2).reshape(TOTAL, D)

    def one_group(items):
        grad_rows, input_rows, pre_rows, query_rows, key_rows, value_rows, frame_lens = items
        resid_grad, ctx_grad, kernel_term, gain_term, seg_own = group_conv(grad_rows, input_rows, pre_rows, frame_lens, norm_gain, kernel, w_in, w_conv_out, w_attn_out)
        query_grad, key_grad, value_grad = lax.map(lambda heads: head_backward(heads[0], heads[1], heads[2], heads[3], seg_own), (split_heads(query_rows), split_heads(key_rows), split_heads(value_rows), split_heads(ctx_grad)))
        return (resid_grad, join_heads(query_grad), join_heads(key_grad), join_heads(value_grad), kernel_term, gain_term)
    groups = (grad_out.reshape(N_DP, TOTAL, D), saved_input.reshape(N_DP, TOTAL, D), pre_glu.reshape(N_DP, TOTAL, 2 * D), queries.reshape(N_DP, TOTAL, D), keys.reshape(N_DP, TOTAL, D), values.reshape(N_DP, TOTAL, D), frame_counts)
    resid_grad, query_grad, key_grad, value_grad, kernel_terms, gain_terms = lax.map(one_group, groups)
    return (resid_grad.reshape(FRAMES, D), query_grad.reshape(FRAMES, D), key_grad.reshape(FRAMES, D), value_grad.reshape(FRAMES, D), lax.optimization_barrier(jnp.sum(kernel_terms, axis=0)), lax.optimization_barrier(jnp.sum(gain_terms, axis=0)))
```

```python
import math

import jax
import jax.numpy as jnp
from jax import lax
from jax.experimental import pallas as pl
from jax.experimental.pallas import tpu as pltpu
from jax.sharding import Mesh
from jax.sharding import PartitionSpec as P

HD = 80
KW = 31
BLK = 256
TIME = ("z", "core")
GROUPS = ("y", "x")


def frame_ends(frame_lens):
    n = frame_lens.shape[0]
    upto = jnp.arange(n)[:, None] >= jnp.arange(n)[None, :]
    return jnp.sum(jnp.where(upto, frame_lens[None, :], 0), axis=1).astype(jnp.int32)


def segments_of(ends, positions):
    counted = jnp.sum((positions[:, None] >= ends[None, :]).astype(jnp.int32), axis=1)
    return jnp.where(positions < 0, jnp.int32(-1), counted)


def padded(block, width):
    count = lax.axis_size(TIME)
    forward = [(i, i + 1) for i in range(count - 1)]
    backward = [(target, source) for source, target in forward]
    low = lax.ppermute(block[block.shape[0] - width :], TIME, forward)
    high = lax.ppermute(block[:width], TIME, backward)
    return jnp.concatenate([low, block, high], axis=0)


def spread(piece, axis):
    count = lax.axis_size(axis)
    copies = jnp.broadcast_to(piece[None], (count,) + piece.shape)
    return lax.all_to_all(copies, axis, split_axis=0, concat_axis=0)


def row_product(active, piece):
    return jnp.einsum("tc,rc->tr", active, piece, preferred_element_type=jnp.float32)


def halves(array, core):
    width = array.shape[1] // 2
    own = lax.dynamic_slice_in_dim(array, core * width, width, 1)
    away = lax.dynamic_slice_in_dim(array, (1 - core) * width, width, 1)
    return own, away


def swap(array):
    return lax.ppermute(array, "core", [(0, 1), (1, 0)])


def pair_product(own, away, piece):
    other = swap(away)
    back = swap(row_product(other, piece))
    return row_product(own, piece) + back


def probs_kernel(bounds, q_t, k, v_t, lo, hi, probs, out_t, inv_sum, scores):
    factor = math.log2(math.e) / math.sqrt(HD)
    block = pl.program_id(0)
    first = bounds[0, block]
    last = bounds[1, block]
    query = q_t[...]
    start = lo[...]
    end = hi[...]
    width = query.shape[1]
    rows = lax.broadcasted_iota(jnp.int32, (BLK, width), 0)

    def score(kb, peak):
        at = pl.multiple_of(kb * BLK, BLK)
        s = jnp.dot(k[pl.ds(at, BLK), :], query, preferred_element_type=jnp.float32)
        valid = (rows >= start - at) & (rows < end - at)
        s = jnp.where(valid, s, -1e30)
        scores[pl.ds(at, BLK), :] = s
        return jnp.maximum(peak, jnp.max(s.reshape(BLK // 8, 8, width), axis=0))

    peak = lax.fori_loop(first, last, score, jnp.full((8, width), -1e30, jnp.float32))
    peak = jnp.max(peak, axis=0, keepdims=True)

    def expo(kb, carry):
        total, acc = carry
        at = pl.multiple_of(kb * BLK, BLK)
        e = jnp.exp2((scores[pl.ds(at, BLK), :] - peak) * factor)
        low = e.astype(jnp.bfloat16)
        probs[pl.ds(at, BLK), :] = low
        acc = acc + jnp.dot(v_t[:, pl.ds(at, BLK)], low, preferred_element_type=jnp.float32)
        return total + jnp.sum(e.reshape(BLK // 8, 8, width), axis=0), acc

    total, acc = lax.fori_loop(
        first,
        last,
        expo,
        (jnp.zeros((8, width), jnp.float32), jnp.zeros((HD, width), jnp.float32)),
    )
    inv = 1.0 / jnp.sum(total, axis=0, keepdims=True)
    inv_sum[...] = inv
    out_t[...] = acc * inv


def attention_probs(bounds, q_t, keys, v_t, lo, hi):
    total = keys.shape[0]
    n = total // BLK
    lanes = lambda rows: pl.BlockSpec((rows, BLK), lambda i, b: (0, i))
    whole = lambda shape: pl.BlockSpec(shape, lambda i, b: (0, 0))
    return pl.pallas_call(
        probs_kernel,
        grid_spec=pltpu.PrefetchScalarGridSpec(
            num_scalar_prefetch=1,
            grid=(n,),
            in_specs=[
                lanes(HD),
                whole((total, HD)),
                whole((HD, total)),
                lanes(1),
                lanes(1),
            ],
            out_specs=[
                pl.BlockSpec((None, total, BLK), lambda i, b: (i, 0, 0)),
                lanes(HD),
                lanes(1),
            ],
            scratch_shapes=[pltpu.VMEM((total, BLK), jnp.float32)],
        ),
        out_shape=[
            jax.ShapeDtypeStruct((n, total, BLK), jnp.bfloat16),
            jax.ShapeDtypeStruct((HD, total), jnp.float32),
            jax.ShapeDtypeStruct((1, total), jnp.float32),
        ],
        compiler_params=pltpu.CompilerParams(vmem_limit_bytes=32 << 20),
        cost_estimate=pl.CostEstimate(
            flops=2 * total * total * HD * 2,
            transcendentals=total * total // 2,
            bytes_accessed=total * total * 2,
        ),
        name="attention_probs",
    )(bounds, q_t, keys, v_t, lo, hi)


def grads_kernel(bounds, probs, ctx_t, out_t, inv_sum, q, k_t, v, dq_t, dk_t, dv_t, dk_acc, dv_acc):
    scale = 1.0 / math.sqrt(HD)
    block = pl.program_id(0)
    first = bounds[0, block]
    last = bounds[1, block]

    @pl.when(block == 0)
    def _():
        dk_acc[...] = jnp.zeros_like(dk_acc)
        dv_acc[...] = jnp.zeros_like(dv_acc)

    pieces = [ctx_t[i].astype(jnp.float32) for i in range(ctx_t.shape[0])]
    grad_t = jnp.concatenate(pieces, axis=1) * inv_sum[...]
    grad_low_t = grad_t.astype(jnp.bfloat16)
    grad_low = grad_t.T.astype(jnp.bfloat16)
    delta = jnp.sum(grad_low_t.astype(jnp.float32) * out_t[...], axis=0, keepdims=True)
    query = q[...]

    def step(kb, acc):
        at = pl.multiple_of(kb * BLK, BLK)
        e = probs[pl.ds(at, BLK), :]
        prob_grad = jnp.dot(v[pl.ds(at, BLK), :], grad_low_t, preferred_element_type=jnp.float32)
        ds = (e.astype(jnp.float32) * (prob_grad - delta)).astype(jnp.bfloat16)
        dv_acc[pl.ds(at, BLK), :] += jnp.dot(e, grad_low, preferred_element_type=jnp.float32)
        dk_acc[pl.ds(at, BLK), :] += jnp.dot(ds, query, preferred_element_type=jnp.float32)
        return acc + jnp.dot(k_t[:, pl.ds(at, BLK)], ds, preferred_element_type=jnp.float32)

    acc = lax.fori_loop(first, last, step, jnp.zeros((HD, query.shape[0]), jnp.float32))
    dq_t[...] = (acc * scale).astype(jnp.bfloat16)

    @pl.when(block == pl.num_programs(0) - 1)
    def _():
        dk_t[...] = (dk_acc[...] * scale).T.astype(jnp.bfloat16)
        dv_t[...] = dv_acc[...].T.astype(jnp.bfloat16)


def attention_grads(bounds, probs, ctx_t, out_t, inv_sum, queries, k_t, values):
    total = queries.shape[0]
    n = total // BLK
    per = BLK // ctx_t.shape[2]
    lanes = lambda rows: pl.BlockSpec((rows, BLK), lambda i, b: (0, i))
    whole = lambda shape: pl.BlockSpec(shape, lambda i, b: (0, 0))
    shape = jax.ShapeDtypeStruct((HD, total), jnp.bfloat16)
    return pl.pallas_call(
        grads_kernel,
        grid_spec=pltpu.PrefetchScalarGridSpec(
            num_scalar_prefetch=1,
            grid=(n,),
            in_specs=[
                pl.BlockSpec((None, total, BLK), lambda i, b: (i, 0, 0)),
                pl.BlockSpec((per, HD, ctx_t.shape[2]), lambda i, b: (i, 0, 0)),
                lanes(HD),
                lanes(1),
                pl.BlockSpec((BLK, HD), lambda i, b: (i, 0)),
                whole((HD, total)),
                whole((total, HD)),
            ],
            out_specs=[lanes(HD), whole((HD, total)), whole((HD, total))],
            scratch_shapes=[pltpu.VMEM((total, HD), jnp.float32)] * 2,
        ),
        out_shape=[shape, shape, shape],
        compiler_params=pltpu.CompilerParams(vmem_limit_bytes=32 << 20),
        cost_estimate=pl.CostEstimate(
            flops=2 * total * total * HD * 4,
            transcendentals=0,
            bytes_accessed=total * total * 2,
        ),
        name="attention_grads",
    )(bounds, probs, ctx_t, out_t, inv_sum, queries, k_t, values)


def local(
    grad_out,
    saved_input,
    pre_glu,
    queries,
    keys,
    values,
    frame_counts,
    norm_gain,
    kernel,
    w_in,
    w_conv_out,
    w_attn_out,
):
    t_dev, width = grad_out.shape
    n_seq = lax.axis_size(TIME)
    total = t_dev * n_seq
    half = KW // 2
    core = lax.axis_index("core")
    ends = frame_ends(frame_counts[0])

    in_low, _ = halves(w_in[:, :width], core)
    in_high, _ = halves(w_in[:, width:], core)
    gathered = lax.all_gather(
        jnp.concatenate([in_low, in_high, w_attn_out], axis=1), GROUPS, axis=0, tiled=True
    )
    w_in_half = gathered[:, :width]
    w_attn = gathered[:, width:]

    conv_half, _ = halves(w_conv_out, core)
    by_y = spread(conv_half, "y")
    by_xy = spread(by_y, "x")
    w_conv_half = by_xy.transpose(1, 0, 2, 3).reshape(width, width // 2)

    positions = jnp.arange(total, dtype=jnp.int32)
    passed = positions[None, :] >= ends[:, None]
    lo = jnp.max(jnp.where(passed, ends[:, None], 0), axis=0, keepdims=True)
    hi = jnp.min(jnp.where(passed, total, ends[:, None]), axis=0, keepdims=True)
    bounds = jnp.stack([lo[0, ::BLK] // BLK, (hi[0, BLK - 1 :: BLK] + BLK - 1) // BLK])
    probs, out_t, inv_sum = attention_probs(bounds, queries.T, keys, values.T, lo, hi)

    seq_index = lax.axis_index(TIME)
    ext_pos = seq_index * t_dev + jnp.arange(-half, t_dev + half, dtype=jnp.int32)
    seg_ext = segments_of(ends, ext_pos)
    seg_own = seg_ext[half : half + t_dev]
    first_half = pre_glu[:, :width].astype(jnp.float32)
    gate_sig = jax.nn.sigmoid(pre_glu[:, width:].astype(jnp.float32))
    glu_out = (first_half * gate_sig).astype(jnp.bfloat16)
    glu_ext = padded(glu_out, half).astype(jnp.float32)
    matches = [
        (seg_ext[tap_index : tap_index + t_dev] == seg_own).astype(jnp.float32)[:, None]
        for tap_index in range(KW)
    ]
    conv_out = jnp.zeros((t_dev, width), jnp.float32)
    for tap_index in range(KW):
        conv_out = (
            conv_out
            + kernel[tap_index] * glu_ext[tap_index : tap_index + t_dev] * matches[tap_index]
        )
    conv_out_grad = pair_product(*halves(grad_out, core), w_conv_half)
    conv_sig = jax.nn.sigmoid(conv_out)
    conv_grad = (conv_out_grad * conv_sig * (1.0 + conv_out * (1.0 - conv_sig))).astype(
        jnp.bfloat16
    )
    grad_ext = padded(conv_grad, half).astype(jnp.float32)
    grad_float = grad_ext[half : half + t_dev]
    glu_grad = jnp.zeros((t_dev, width), jnp.float32)
    kernel_rows = []
    for tap_index in range(KW):
        back = 2 * half - tap_index
        glu_grad = glu_grad + kernel[tap_index] * grad_ext[back : back + t_dev] * matches[back]
        kernel_rows.append(
            jnp.sum(
                grad_float * glu_ext[tap_index : tap_index + t_dev] * matches[tap_index], axis=0
            )
        )
    low_grad = (glu_grad * gate_sig).astype(jnp.bfloat16)
    high_grad = (glu_grad * first_half * gate_sig * (1.0 - gate_sig)).astype(jnp.bfloat16)
    low_own, low_away = halves(low_grad, core)
    high_own, high_away = halves(high_grad, core)

    rows = jnp.stack(kernel_rows + [jnp.zeros((width,), jnp.float32)])
    rows = lax.all_to_all(
        rows.reshape(n_seq, (KW + 1) // n_seq, width), TIME, split_axis=0, concat_axis=0
    )
    rows = jnp.sum(rows, axis=0)
    for axis in GROUPS:
        rows = jnp.sum(spread(rows, axis), axis=0)
    kernel_grad = spread(rows, TIME).reshape(KW + 1, width)[:KW]

    norm_grad = pair_product(
        jnp.concatenate([low_own, high_own], axis=1),
        jnp.concatenate([low_away, high_away], axis=1),
        w_in_half,
    )
    inputs = saved_input.astype(jnp.float32)
    centred = inputs - jnp.mean(inputs, axis=1, keepdims=True)
    inv_std = 1.0 / jnp.sqrt(jnp.mean(centred * centred, axis=1, keepdims=True) + 1e-05)
    normed = centred * inv_std
    scaled_grad = norm_grad * norm_gain
    input_grad = inv_std * (
        scaled_grad
        - jnp.mean(scaled_grad, axis=1, keepdims=True)
        - normed * jnp.mean(scaled_grad * normed, axis=1, keepdims=True)
    )
    resid_grad = (grad_out.astype(jnp.float32) + input_grad).astype(jnp.bfloat16)
    ctx_t = jnp.einsum("rc,tc->rt", w_attn, resid_grad, preferred_element_type=jnp.float32)
    ctx_t = ctx_t.astype(jnp.bfloat16).reshape(n_seq, HD, t_dev)
    ctx_t = lax.all_to_all(ctx_t, TIME, split_axis=0, concat_axis=0)
    grads = attention_grads(
        bounds, probs, ctx_t, out_t, inv_sum, queries, keys.T, values
    )
    query_grad, key_grad, value_grad = [array.T for array in grads]
    gain = jnp.sum(norm_grad * normed, axis=0, keepdims=True)
    for axis in (TIME,) + GROUPS:
        gain = jnp.sum(spread(gain, axis), axis=0)
    return (resid_grad, query_grad, key_grad, value_grad, kernel_grad, gain[0])


def solution(mesh):
    dp, seq = mesh.devices.shape
    shape = (dp // 4, 4, seq // 2, 2)
    fine = Mesh(mesh.devices.reshape(shape), GROUPS + TIME)
    frames = P(GROUPS + TIME, None)
    heads = P(GROUPS, TIME)
    group = P(GROUPS, None)
    in_specs = (
        frames,
        frames,
        frames,
        heads,
        heads,
        heads,
        group,
        P(),
        P(),
        group,
        group,
        group,
    )
    out_specs = (frames, heads, heads, heads, P(), P())
    return jax.shard_map(local, mesh=fine, in_specs=in_specs, out_specs=out_specs, check_vma=False)
```

```python
import math

import jax
import jax.numpy as jnp
from jax import lax
from jax.experimental import pallas as pl
from jax.experimental.pallas import tpu as pltpu
from jax.sharding import Mesh
from jax.sharding import PartitionSpec as P

HD = 80
KW = 31
BLK = 256
TIME = ("z", "core")
GROUPS = ("y", "x")


def frame_ends(frame_lens):
    n = frame_lens.shape[0]
    upto = jnp.arange(n)[:, None] >= jnp.arange(n)[None, :]
    return jnp.sum(jnp.where(upto, frame_lens[None, :], 0), axis=1).astype(jnp.int32)


def segments_of(ends, positions):
    counted = jnp.sum((positions[:, None] >= ends[None, :]).astype(jnp.int32), axis=1)
    return jnp.where(positions < 0, jnp.int32(-1), counted)


def padded(block, width):
    count = lax.axis_size(TIME)
    forward = [(i, i + 1) for i in range(count - 1)]
    backward = [(target, source) for source, target in forward]
    low = lax.ppermute(block[block.shape[0] - width :], TIME, forward)
    high = lax.ppermute(block[:width], TIME, backward)
    return jnp.concatenate([low, block, high], axis=0)


def spread(piece, axis):
    count = lax.axis_size(axis)
    copies = jnp.broadcast_to(piece[None], (count,) + piece.shape)
    return lax.all_to_all(copies, axis, split_axis=0, concat_axis=0)


def row_product(active, piece):
    return jnp.einsum("tc,rc->tr", active, piece, preferred_element_type=jnp.float32)


def halves(array, core):
    width = array.shape[1] // 2
    own = lax.dynamic_slice_in_dim(array, core * width, width, 1)
    away = lax.dynamic_slice_in_dim(array, (1 - core) * width, width, 1)
    return own, away


def swap(array):
    return lax.ppermute(array, "core", [(0, 1), (1, 0)])


def pair_product(own, away, piece):
    other = swap(away)
    back = swap(row_product(other, piece).astype(jnp.bfloat16))
    return row_product(own, piece) + back.astype(jnp.float32)


def probs_kernel(bounds, q_t, k, v_t, lo, hi, probs, out_t, inv_sum, scores):
    factor = math.log2(math.e) / math.sqrt(HD)
    block = pl.program_id(0)
    first = bounds[0, block]
    last = bounds[1, block]
    query = q_t[...]
    start = lo[...]
    end = hi[...]
    width = query.shape[1]
    rows = lax.broadcasted_iota(jnp.int32, (BLK, width), 0)

    def score(kb, peak):
        at = pl.multiple_of(kb * BLK, BLK)
        s = jnp.dot(k[pl.ds(at, BLK), :], query, preferred_element_type=jnp.float32)
        valid = (rows >= start - at) & (rows < end - at)
        s = jnp.where(valid, s, -1e30)
        scores[pl.ds(at, BLK), :] = s
        return jnp.maximum(peak, jnp.max(s.reshape(BLK // 8, 8, width), axis=0))

    peak = lax.fori_loop(first, last, score, jnp.full((8, width), -1e30, jnp.float32))
    peak = jnp.max(peak, axis=0, keepdims=True)

    def expo(kb, carry):
        total, acc = carry
        at = pl.multiple_of(kb * BLK, BLK)
        e = jnp.exp2((scores[pl.ds(at, BLK), :] - peak) * factor)
        low = e.astype(jnp.bfloat16)
        probs[pl.ds(at, BLK), :] = low
        acc = acc + jnp.dot(v_t[:, pl.ds(at, BLK)], low, preferred_element_type=jnp.float32)
        return total + jnp.sum(e.reshape(BLK // 8, 8, width), axis=0), acc

    total, acc = lax.fori_loop(
        first,
        last,
        expo,
        (jnp.zeros((8, width), jnp.float32), jnp.zeros((HD, width), jnp.float32)),
    )
    inv = 1.0 / jnp.sum(total, axis=0, keepdims=True)
    inv_sum[...] = inv
    out_t[...] = acc * inv


def attention_probs(bounds, q_t, keys, v_t, lo, hi):
    total = keys.shape[0]
    n = total // BLK
    lanes = lambda rows: pl.BlockSpec((rows, BLK), lambda i, b: (0, i))
    whole = lambda shape: pl.BlockSpec(shape, lambda i, b: (0, 0))
    return pl.pallas_call(
        probs_kernel,
        grid_spec=pltpu.PrefetchScalarGridSpec(
            num_scalar_prefetch=1,
            grid=(n,),
            in_specs=[
                lanes(HD),
                whole((total, HD)),
                whole((HD, total)),
                lanes(1),
                lanes(1),
            ],
            out_specs=[
                pl.BlockSpec((None, total, BLK), lambda i, b: (i, 0, 0)),
                lanes(HD),
                lanes(1),
            ],
            scratch_shapes=[pltpu.VMEM((total, BLK), jnp.float32)],
        ),
        out_shape=[
            jax.ShapeDtypeStruct((n, total, BLK), jnp.bfloat16),
            jax.ShapeDtypeStruct((HD, total), jnp.float32),
            jax.ShapeDtypeStruct((1, total), jnp.float32),
        ],
        compiler_params=pltpu.CompilerParams(vmem_limit_bytes=32 << 20),
        cost_estimate=pl.CostEstimate(
            flops=2 * total * total * HD * 2,
            transcendentals=total * total // 2,
            bytes_accessed=total * total * 2,
        ),
        name="attention_probs",
    )(bounds, q_t, keys, v_t, lo, hi)


def grads_kernel(begin, bounds, probs, ctx_t, out_t, inv_sum, q, k_t, v, *refs):
    carried = begin > 0
    dk_in, dv_in = refs[:2] if carried else (None, None)
    dq_t, dk_t, dv_t, dk_acc, dv_acc = refs[-5:]
    scale = 1.0 / math.sqrt(HD)
    step_id = pl.program_id(0)
    first = bounds[0, begin + step_id]
    last = bounds[1, begin + step_id]

    @pl.when(step_id == 0)
    def _():
        dk_acc[...] = dk_in[...] if carried else jnp.zeros_like(dk_acc)
        dv_acc[...] = dv_in[...] if carried else jnp.zeros_like(dv_acc)

    pieces = [ctx_t[i].astype(jnp.float32) for i in range(ctx_t.shape[0])]
    grad_t = jnp.concatenate(pieces, axis=1) * inv_sum[...]
    grad_low_t = grad_t.astype(jnp.bfloat16)
    grad_low = grad_t.T.astype(jnp.bfloat16)
    delta = jnp.sum(grad_low_t.astype(jnp.float32) * out_t[...], axis=0, keepdims=True)
    query = q[...]

    def step(kb, acc):
        at = pl.multiple_of(kb * BLK, BLK)
        e = probs[pl.ds(at, BLK), :]
        prob_grad = jnp.dot(v[pl.ds(at, BLK), :], grad_low_t, preferred_element_type=jnp.float32)
        ds = (e.astype(jnp.float32) * (prob_grad - delta)).astype(jnp.bfloat16)
        dv_acc[pl.ds(at, BLK), :] += jnp.dot(e, grad_low, preferred_element_type=jnp.float32)
        dk_acc[pl.ds(at, BLK), :] += jnp.dot(ds, query, preferred_element_type=jnp.float32)
        return acc + jnp.dot(k_t[:, pl.ds(at, BLK)], ds, preferred_element_type=jnp.float32)

    acc = lax.fori_loop(first, last, step, jnp.zeros((HD, query.shape[0]), jnp.float32))
    dq_t[...] = (acc * scale).astype(jnp.bfloat16)

    @pl.when(step_id == pl.num_programs(0) - 1)
    def _():
        if dk_t.shape[0] == HD:
            dk_t[...] = (dk_acc[...] * scale).T.astype(jnp.bfloat16)
            dv_t[...] = dv_acc[...].T.astype(jnp.bfloat16)
        else:
            dk_t[...] = dk_acc[...]
            dv_t[...] = dv_acc[...]


def attention_grads(begin, end, bounds, probs, ctx_t, out_t, inv_sum, queries, k_t, values, *sums):
    total = queries.shape[0]
    n = total // BLK
    per = BLK // ctx_t.shape[2]
    lanes = lambda rows: pl.BlockSpec((rows, BLK), lambda i, b: (0, i + begin))
    whole = lambda shape: pl.BlockSpec(shape, lambda i, b: (0, 0))
    if end == n:
        shape = jax.ShapeDtypeStruct((HD, total), jnp.bfloat16)
    else:
        shape = jax.ShapeDtypeStruct((total, HD), jnp.float32)
    return pl.pallas_call(
        lambda *refs: grads_kernel(begin, *refs),
        grid_spec=pltpu.PrefetchScalarGridSpec(
            num_scalar_prefetch=1,
            grid=(end - begin,),
            in_specs=[
                pl.BlockSpec((None, total, BLK), lambda i, b: (i + begin, 0, 0)),
                pl.BlockSpec((per, HD, ctx_t.shape[2]), lambda i, b: (i + begin, 0, 0)),
                lanes(HD),
                lanes(1),
                pl.BlockSpec((BLK, HD), lambda i, b: (i + begin, 0)),
                whole((HD, total)),
                whole((total, HD)),
            ]
            + [whole((total, HD))] * len(sums),
            out_specs=[
                pl.BlockSpec((HD, BLK), lambda i, b: (0, i)),
                whole(shape.shape),
                whole(shape.shape),
            ],
            scratch_shapes=[pltpu.VMEM((total, HD), jnp.float32)] * 2,
        ),
        out_shape=[
            jax.ShapeDtypeStruct((HD, (end - begin) * BLK), jnp.bfloat16),
            shape,
            shape,
        ],
        compiler_params=pltpu.CompilerParams(vmem_limit_bytes=32 << 20),
        cost_estimate=pl.CostEstimate(
            flops=2 * total * BLK * (end - begin) * HD * 4,
            transcendentals=0,
            bytes_accessed=total * BLK * (end - begin) * 2,
        ),
        name="attention_grads",
    )(bounds, probs, ctx_t, out_t, inv_sum, queries, k_t, values, *sums)


def local(
    grad_out,
    saved_input,
    pre_glu,
    queries,
    keys,
    values,
    frame_counts,
    norm_gain,
    kernel,
    w_in,
    w_conv_out,
    w_attn_out,
):
    t_dev, width = grad_out.shape
    n_seq = lax.axis_size(TIME)
    total = t_dev * n_seq
    half = KW // 2
    core = lax.axis_index("core")
    ends = frame_ends(frame_counts[0])

    in_low, _ = halves(w_in[:, :width], core)
    in_high, _ = halves(w_in[:, width:], core)
    gathered = lax.all_gather(
        jnp.concatenate([in_low, in_high, w_attn_out], axis=1), GROUPS, axis=0, tiled=True
    )

    positions = jnp.arange(total, dtype=jnp.int32)
    passed = positions[None, :] >= ends[:, None]
    lo = jnp.max(jnp.where(passed, ends[:, None], 0), axis=0, keepdims=True)
    hi = jnp.min(jnp.where(passed, total, ends[:, None]), axis=0, keepdims=True)
    bounds = jnp.stack([lo[0, ::BLK] // BLK, (hi[0, BLK - 1 :: BLK] + BLK - 1) // BLK])

    conv_half, _ = halves(w_conv_out, core)
    by_y = spread(conv_half, "y")
    by_y, lo = lax.optimization_barrier((by_y, lo))
    by_xy = spread(by_y, "x")
    probs, out_t, inv_sum = attention_probs(bounds, queries.T, keys, values.T, lo, hi)
    by_xy, probs = lax.optimization_barrier((by_xy, probs))
    w_conv_half = by_xy.transpose(1, 0, 2, 3).reshape(width, width // 2)

    seq_index = lax.axis_index(TIME)
    ext_pos = seq_index * t_dev + jnp.arange(-half, t_dev + half, dtype=jnp.int32)
    seg_ext = segments_of(ends, ext_pos)
    seg_own = seg_ext[half : half + t_dev]
    first_half = pre_glu[:, :width].astype(jnp.float32)
    gate_sig = jax.nn.sigmoid(pre_glu[:, width:].astype(jnp.float32))
    glu_out = (first_half * gate_sig).astype(jnp.bfloat16)
    glu_ext = padded(glu_out, half).astype(jnp.float32)
    matches = [
        (seg_ext[tap_index : tap_index + t_dev] == seg_own).astype(jnp.float32)[:, None]
        for tap_index in range(KW)
    ]
    conv_out = jnp.zeros((t_dev, width), jnp.float32)
    for tap_index in range(KW):
        conv_out = (
            conv_out
            + kernel[tap_index] * glu_ext[tap_index : tap_index + t_dev] * matches[tap_index]
        )
    conv_out_grad = pair_product(*halves(grad_out, core), w_conv_half)
    conv_sig = jax.nn.sigmoid(conv_out)
    conv_grad = (conv_out_grad * conv_sig * (1.0 + conv_out * (1.0 - conv_sig))).astype(
        jnp.bfloat16
    )
    grad_ext = padded(conv_grad, half).astype(jnp.float32)
    grad_float = grad_ext[half : half + t_dev]
    glu_grad = jnp.zeros((t_dev, width), jnp.float32)
    kernel_rows = []
    for tap_index in range(KW):
        back = 2 * half - tap_index
        glu_grad = glu_grad + kernel[tap_index] * grad_ext[back : back + t_dev] * matches[back]
        kernel_rows.append(
            jnp.sum(
                grad_float * glu_ext[tap_index : tap_index + t_dev] * matches[tap_index], axis=0
            )
        )
    low_grad = (glu_grad * gate_sig).astype(jnp.bfloat16)
    high_grad = (glu_grad * first_half * gate_sig * (1.0 - gate_sig)).astype(jnp.bfloat16)
    low_own, low_away = halves(low_grad, core)
    high_own, high_away = halves(high_grad, core)

    rows = jnp.stack(kernel_rows + [jnp.zeros((width,), jnp.float32)])
    rows = lax.all_to_all(
        rows.reshape(n_seq, (KW + 1) // n_seq, width), TIME, split_axis=0, concat_axis=0
    )
    rows = jnp.sum(rows, axis=0)

    gathered, rows = lax.optimization_barrier((gathered, rows))
    w_in_half = gathered[:, :width]
    w_attn = gathered[:, width:]
    norm_grad = pair_product(
        jnp.concatenate([low_own, high_own], axis=1),
        jnp.concatenate([low_away, high_away], axis=1),
        w_in_half,
    )
    inputs = saved_input.astype(jnp.float32)
    centred = inputs - jnp.mean(inputs, axis=1, keepdims=True)
    inv_std = 1.0 / jnp.sqrt(jnp.mean(centred * centred, axis=1, keepdims=True) + 1e-05)
    normed = centred * inv_std
    scaled_grad = norm_grad * norm_gain
    input_grad = inv_std * (
        scaled_grad
        - jnp.mean(scaled_grad, axis=1, keepdims=True)
        - normed * jnp.mean(scaled_grad * normed, axis=1, keepdims=True)
    )
    resid_grad = (grad_out.astype(jnp.float32) + input_grad).astype(jnp.bfloat16)
    ctx_t = jnp.einsum("rc,tc->rt", w_attn, resid_grad, preferred_element_type=jnp.float32)
    ctx_t = ctx_t.astype(jnp.bfloat16).reshape(n_seq, HD, t_dev)
    gain = jnp.sum(norm_grad * normed, axis=0, keepdims=True)
    ctx_t, gain = lax.optimization_barrier((ctx_t, gain))
    ctx_t = lax.all_to_all(ctx_t, TIME, split_axis=0, concat_axis=0)
    sums = jnp.concatenate([rows, gain], axis=0)
    fixed = (bounds, probs, ctx_t, out_t, inv_sum, queries, keys.T, values)
    n = total // BLK
    cuts = [0, 3 * n // 8, 6 * n // 8, n]
    parts = []
    acc = ()
    for stage, axis in enumerate(GROUPS + (TIME,)):
        stacked = spread(sums, axis)
        part, *acc = attention_grads(cuts[stage], cuts[stage + 1], *fixed, *acc)
        parts.append(part)
        if stage < 2:
            stacked, *acc = lax.optimization_barrier((stacked, *acc))
            sums = jnp.sum(stacked, axis=0)
    query_grad = jnp.concatenate(parts, axis=1).T
    key_grad, value_grad = [array.T for array in acc]
    kernel_grad = stacked[:, :-1].reshape(KW + 1, width)[:KW]
    gain_grad = jnp.sum(stacked[:, -1], axis=0)
    return (resid_grad, query_grad, key_grad, value_grad, kernel_grad, gain_grad)


def solution(mesh):
    dp, seq = mesh.devices.shape
    shape = (dp // 4, 4, seq // 2, 2)
    fine = Mesh(mesh.devices.reshape(shape), GROUPS + TIME)
    frames = P(GROUPS + TIME, None)
    heads = P(GROUPS, TIME)
    group = P(GROUPS, None)
    in_specs = (
        frames,
        frames,
        frames,
        heads,
        heads,
        heads,
        group,
        P(),
        P(),
        group,
        group,
        group,
    )
    out_specs = (frames, heads, heads, heads, P(), P())
    return jax.shard_map(local, mesh=fine, in_specs=in_specs, out_specs=out_specs, check_vma=False)
```

```python
import math

import jax
import jax.numpy as jnp
from jax import lax
from jax.experimental import pallas as pl
from jax.experimental.pallas import tpu as pltpu
from jax.sharding import Mesh
from jax.sharding import PartitionSpec as P

HD = 80
KW = 31
BLK = 256
HALO = 16
LANES = 128
TIME = ("z", "core")
GROUPS = ("y", "x")


def frame_ends(frame_lens):
    n = frame_lens.shape[0]
    upto = jnp.arange(n)[:, None] >= jnp.arange(n)[None, :]
    return jnp.sum(jnp.where(upto, frame_lens[None, :], 0), axis=1).astype(jnp.int32)


def segments_of(ends, positions):
    counted = jnp.sum((positions[:, None] >= ends[None, :]).astype(jnp.int32), axis=1)
    return jnp.where(positions < 0, jnp.int32(-1), counted)


def padded(block, width):
    count = lax.axis_size(TIME)
    forward = [(i, i + 1) for i in range(count - 1)]
    backward = [(target, source) for source, target in forward]
    low = lax.ppermute(block[block.shape[0] - width :], TIME, forward)
    high = lax.ppermute(block[:width], TIME, backward)
    return jnp.concatenate([low, block, high], axis=0)


def spread(piece, axis):
    count = lax.axis_size(axis)
    copies = jnp.broadcast_to(piece[None], (count,) + piece.shape)
    return lax.all_to_all(copies, axis, split_axis=0, concat_axis=0)


def row_product(active, piece):
    return jnp.einsum("tc,rc->tr", active, piece, preferred_element_type=jnp.float32)


def halves(array, core):
    width = array.shape[1] // 2
    own = lax.dynamic_slice_in_dim(array, core * width, width, 1)
    away = lax.dynamic_slice_in_dim(array, (1 - core) * width, width, 1)
    return own, away


def swap(array):
    return lax.ppermute(array, "core", [(0, 1), (1, 0)])


def pair_product(own, away, piece):
    other = swap(away)
    back = swap(row_product(other, piece).astype(jnp.bfloat16))
    return row_product(own, piece) + back.astype(jnp.float32)


def fill_matches(seg, matches):
    rows = matches.shape[1]
    own = seg[pl.ds(HALO, rows), :]
    for tap in range(KW):
        there = seg[pl.ds(tap + HALO - KW // 2, rows), :]
        matches[tap] = jnp.where(there == own, 1.0, 0.0)


def conv_kernel(seg, glu, taps, factor, matches, wide):
    rows = factor.shape[0]

    @pl.when(pl.program_id(0) == 0)
    def _():
        fill_matches(seg, matches)

    wide[...] = glu[...].astype(jnp.float32)
    out = jnp.zeros(factor.shape, jnp.float32)
    for tap in range(KW):
        seen = wide[pl.ds(tap + HALO - KW // 2, rows), :] * matches[tap]
        out = out + taps[pl.ds(tap, 1), :] * seen
    sig = 1.0 / (1.0 + jnp.exp(-out))
    factor[...] = sig * (1.0 + out * (1.0 - sig))


def conv_factor(seg, glu_ext, taps):
    ext, width = glu_ext.shape
    rows = ext - 2 * HALO
    lanes = lambda count: pl.BlockSpec((count, LANES), lambda i: (0, i))
    return pl.pallas_call(
        conv_kernel,
        grid=(width // LANES,),
        in_specs=[pl.BlockSpec((ext, LANES), lambda i: (0, 0)), lanes(ext), lanes(KW)],
        out_specs=lanes(rows),
        out_shape=jax.ShapeDtypeStruct((rows, width), jnp.float32),
        scratch_shapes=[
            pltpu.VMEM((KW, rows, LANES), jnp.float32),
            pltpu.VMEM((ext, LANES), jnp.float32),
        ],
        compiler_params=pltpu.CompilerParams(vmem_limit_bytes=10 << 20),
        cost_estimate=pl.CostEstimate(
            flops=4 * KW * rows * width, transcendentals=rows * width, bytes_accessed=8 * rows * width
        ),
        name="conv_factor",
    )(seg, glu_ext, taps)


def conv_grads_kernel(
    seg, grad, glu, first_ref, gate_ref, taps, low, high, tap_grad, matches, wide_grad, wide_glu
):
    rows = low.shape[0]

    @pl.when(pl.program_id(0) == 0)
    def _():
        fill_matches(seg, matches)

    wide_grad[...] = grad[...].astype(jnp.float32)
    wide_glu[...] = glu[...].astype(jnp.float32)
    own = wide_grad[pl.ds(HALO, rows), :]
    glu_grad = jnp.zeros(low.shape, jnp.float32)
    for tap in range(KW):
        at = pl.ds(tap + HALO - KW // 2, rows)
        match = matches[tap]
        glu_grad = glu_grad + taps[pl.ds(KW - 1 - tap, 1), :] * (wide_grad[at, :] * match)
        tap_grad[pl.ds(tap, 1), :] = jnp.sum(own * (wide_glu[at, :] * match), axis=0, keepdims=True)
    tap_grad[pl.ds(KW, 1), :] = jnp.zeros((1, LANES), jnp.float32)
    first = first_ref[...].astype(jnp.float32)
    sig = 1.0 / (1.0 + jnp.exp(-gate_ref[...].astype(jnp.float32)))
    part = glu_grad * sig
    low[...] = part.astype(jnp.bfloat16)
    high[...] = (part * first * (1.0 - sig)).astype(jnp.bfloat16)


def conv_grads(seg, grad_ext, glu_ext, pre_glu, taps):
    ext, width = glu_ext.shape
    rows = ext - 2 * HALO
    n = width // LANES
    lanes = lambda count: pl.BlockSpec((count, LANES), lambda i: (0, i))
    return pl.pallas_call(
        conv_grads_kernel,
        grid=(n,),
        in_specs=[
            pl.BlockSpec((ext, LANES), lambda i: (0, 0)),
            lanes(ext),
            lanes(ext),
            lanes(rows),
            pl.BlockSpec((rows, LANES), lambda i: (0, i + n)),
            lanes(KW),
        ],
        out_specs=[lanes(rows), lanes(rows), lanes(KW + 1)],
        out_shape=[
            jax.ShapeDtypeStruct((rows, width), jnp.bfloat16),
            jax.ShapeDtypeStruct((rows, width), jnp.bfloat16),
            jax.ShapeDtypeStruct((KW + 1, width), jnp.float32),
        ],
        scratch_shapes=[
            pltpu.VMEM((KW, rows, LANES), jnp.float32),
            pltpu.VMEM((ext, LANES), jnp.float32),
            pltpu.VMEM((ext, LANES), jnp.float32),
        ],
        compiler_params=pltpu.CompilerParams(vmem_limit_bytes=10 << 20),
        cost_estimate=pl.CostEstimate(
            flops=8 * KW * rows * width, transcendentals=rows * width, bytes_accessed=16 * rows * width
        ),
        name="conv_grads",
    )(seg, grad_ext, glu_ext, pre_glu, pre_glu, taps)


def probs_kernel(bounds, q_t, k, v_t, lo, hi, probs, out_t, inv_sum, scores):
    factor = math.log2(math.e) / math.sqrt(HD)
    block = pl.program_id(0)
    first = bounds[0, block]
    last = bounds[1, block]
    query = q_t[...]
    start = lo[...]
    end = hi[...]
    width = query.shape[1]
    rows = lax.broadcasted_iota(jnp.int32, (BLK, width), 0)

    def score(kb, peak):
        at = pl.multiple_of(kb * BLK, BLK)
        s = jnp.dot(k[pl.ds(at, BLK), :], query, preferred_element_type=jnp.float32)
        valid = (rows >= start - at) & (rows < end - at)
        s = jnp.where(valid, s, -1e30)
        scores[pl.ds(at, BLK), :] = s
        return jnp.maximum(peak, jnp.max(s.reshape(BLK // 8, 8, width), axis=0))

    peak = lax.fori_loop(first, last, score, jnp.full((8, width), -1e30, jnp.float32))
    peak = jnp.max(peak, axis=0, keepdims=True)

    def expo(kb, carry):
        total, acc = carry
        at = pl.multiple_of(kb * BLK, BLK)
        e = jnp.exp2((scores[pl.ds(at, BLK), :] - peak) * factor)
        low = e.astype(jnp.bfloat16)
        probs[pl.ds(at, BLK), :] = low
        acc = acc + jnp.dot(v_t[:, pl.ds(at, BLK)], low, preferred_element_type=jnp.float32)
        return total + jnp.sum(e.reshape(BLK // 8, 8, width), axis=0), acc

    total, acc = lax.fori_loop(
        first,
        last,
        expo,
        (jnp.zeros((8, width), jnp.float32), jnp.zeros((HD, width), jnp.float32)),
    )
    inv = 1.0 / jnp.sum(total, axis=0, keepdims=True)
    inv_sum[...] = inv
    out_t[...] = acc * inv


def attention_probs(bounds, q_t, keys, v_t, lo, hi):
    total = keys.shape[0]
    n = total // BLK
    lanes = lambda rows: pl.BlockSpec((rows, BLK), lambda i, b: (0, i))
    whole = lambda shape: pl.BlockSpec(shape, lambda i, b: (0, 0))
    return pl.pallas_call(
        probs_kernel,
        grid_spec=pltpu.PrefetchScalarGridSpec(
            num_scalar_prefetch=1,
            grid=(n,),
            in_specs=[
                lanes(HD),
                whole((total, HD)),
                whole((HD, total)),
                lanes(1),
                lanes(1),
            ],
            out_specs=[
                pl.BlockSpec((None, total, BLK), lambda i, b: (i, 0, 0)),
                lanes(HD),
                lanes(1),
            ],
            scratch_shapes=[pltpu.VMEM((total, BLK), jnp.float32)],
        ),
        out_shape=[
            pltpu.HBM((n, total, BLK), jnp.bfloat16),
            jax.ShapeDtypeStruct((HD, total), jnp.float32),
            jax.ShapeDtypeStruct((1, total), jnp.float32),
        ],
        compiler_params=pltpu.CompilerParams(vmem_limit_bytes=14 << 20),
        cost_estimate=pl.CostEstimate(
            flops=2 * total * total * HD * 2,
            transcendentals=total * total // 2,
            bytes_accessed=total * total * 2,
        ),
        name="attention_probs",
    )(bounds, q_t, keys, v_t, lo, hi)


def grads_kernel(begin, bounds, probs, ctx_t, out_t, inv_sum, q, k_t, v, *refs):
    carried = begin > 0
    dk_in, dv_in = refs[:2] if carried else (None, None)
    dq_t, dk_t, dv_t, dk_acc, dv_acc = refs[-5:]
    scale = 1.0 / math.sqrt(HD)
    step_id = pl.program_id(0)
    first = bounds[0, begin + step_id]
    last = bounds[1, begin + step_id]

    @pl.when(step_id == 0)
    def _():
        dk_acc[...] = dk_in[...] if carried else jnp.zeros_like(dk_acc)
        dv_acc[...] = dv_in[...] if carried else jnp.zeros_like(dv_acc)

    pieces = [ctx_t[i].astype(jnp.float32) for i in range(ctx_t.shape[0])]
    grad_t = jnp.concatenate(pieces, axis=1) * inv_sum[...]
    grad_low_t = grad_t.astype(jnp.bfloat16)
    grad_low = grad_t.T.astype(jnp.bfloat16)
    delta = jnp.sum(grad_low_t.astype(jnp.float32) * out_t[...], axis=0, keepdims=True)
    query = q[...]

    def step(kb, acc):
        at = pl.multiple_of(kb * BLK, BLK)
        e = probs[pl.ds(at, BLK), :]
        prob_grad = jnp.dot(v[pl.ds(at, BLK), :], grad_low_t, preferred_element_type=jnp.float32)
        ds = (e.astype(jnp.float32) * (prob_grad - delta)).astype(jnp.bfloat16)
        dv_acc[pl.ds(at, BLK), :] += jnp.dot(e, grad_low, preferred_element_type=jnp.float32)
        dk_acc[pl.ds(at, BLK), :] += jnp.dot(ds, query, preferred_element_type=jnp.float32)
        return acc + jnp.dot(k_t[:, pl.ds(at, BLK)], ds, preferred_element_type=jnp.float32)

    acc = lax.fori_loop(first, last, step, jnp.zeros((HD, query.shape[0]), jnp.float32))
    dq_t[...] = (acc * scale).astype(jnp.bfloat16)

    @pl.when(step_id == pl.num_programs(0) - 1)
    def _():
        if dk_t.shape[0] == HD:
            dk_t[...] = (dk_acc[...] * scale).T.astype(jnp.bfloat16)
            dv_t[...] = dv_acc[...].T.astype(jnp.bfloat16)
        else:
            dk_t[...] = dk_acc[...]
            dv_t[...] = dv_acc[...]


def attention_grads(begin, end, bounds, probs, ctx_t, out_t, inv_sum, queries, k_t, values, *sums):
    total = queries.shape[0]
    n = total // BLK
    per = BLK // ctx_t.shape[2]
    lanes = lambda rows: pl.BlockSpec((rows, BLK), lambda i, b: (0, i + begin))
    whole = lambda shape: pl.BlockSpec(shape, lambda i, b: (0, 0))
    if end == n:
        shape = jax.ShapeDtypeStruct((HD, total), jnp.bfloat16)
    else:
        shape = jax.ShapeDtypeStruct((total, HD), jnp.float32)
    return pl.pallas_call(
        lambda *refs: grads_kernel(begin, *refs),
        grid_spec=pltpu.PrefetchScalarGridSpec(
            num_scalar_prefetch=1,
            grid=(end - begin,),
            in_specs=[
                pl.BlockSpec((None, total, BLK), lambda i, b: (i + begin, 0, 0)),
                pl.BlockSpec((per, HD, ctx_t.shape[2]), lambda i, b: (i + begin, 0, 0)),
                lanes(HD),
                lanes(1),
                pl.BlockSpec((BLK, HD), lambda i, b: (i + begin, 0)),
                whole((HD, total)),
                whole((total, HD)),
            ]
            + [whole((total, HD))] * len(sums),
            out_specs=[
                pl.BlockSpec((HD, BLK), lambda i, b: (0, i)),
                whole(shape.shape),
                whole(shape.shape),
            ],
            scratch_shapes=[pltpu.VMEM((total, HD), jnp.float32)] * 2,
        ),
        out_shape=[
            jax.ShapeDtypeStruct((HD, (end - begin) * BLK), jnp.bfloat16),
            shape,
            shape,
        ],
        compiler_params=pltpu.CompilerParams(vmem_limit_bytes=18 << 20),
        cost_estimate=pl.CostEstimate(
            flops=2 * total * BLK * (end - begin) * HD * 4,
            transcendentals=0,
            bytes_accessed=total * BLK * (end - begin) * 2,
        ),
        name="attention_grads",
    )(bounds, probs, ctx_t, out_t, inv_sum, queries, k_t, values, *sums)


def local(
    grad_out,
    saved_input,
    pre_glu,
    queries,
    keys,
    values,
    frame_counts,
    norm_gain,
    kernel,
    w_in,
    w_conv_out,
    w_attn_out,
):
    t_dev, width = grad_out.shape
    n_seq = lax.axis_size(TIME)
    total = t_dev * n_seq
    core = lax.axis_index("core")
    ends = frame_ends(frame_counts[0])

    in_low, _ = halves(w_in[:, :width], core)
    in_high, _ = halves(w_in[:, width:], core)
    gathered = lax.all_gather(
        jnp.concatenate([in_low, in_high, w_attn_out], axis=1), GROUPS, axis=0, tiled=True
    )

    positions = jnp.arange(total, dtype=jnp.int32)
    passed = positions[None, :] >= ends[:, None]
    lo = jnp.max(jnp.where(passed, ends[:, None], 0), axis=0, keepdims=True)
    hi = jnp.min(jnp.where(passed, total, ends[:, None]), axis=0, keepdims=True)
    bounds = jnp.stack([lo[0, ::BLK] // BLK, (hi[0, BLK - 1 :: BLK] + BLK - 1) // BLK])

    conv_half, _ = halves(w_conv_out, core)
    by_y = spread(conv_half, "y")
    ext_pos = lax.axis_index(TIME) * t_dev + jnp.arange(-HALO, t_dev + HALO, dtype=jnp.int32)
    seg_ext = jnp.broadcast_to(segments_of(ends, ext_pos)[:, None], (t_dev + 2 * HALO, LANES))
    gate_sig = jax.nn.sigmoid(pre_glu[:, width:].astype(jnp.float32))
    glu_out = (pre_glu[:, :width].astype(jnp.float32) * gate_sig).astype(jnp.bfloat16)
    glu_ext = padded(glu_out, HALO)
    by_y, lo = lax.optimization_barrier((by_y, lo))
    by_xy = spread(by_y, "x")
    probs, out_t, inv_sum = attention_probs(bounds, queries.T, keys, values.T, lo, hi)
    factor = conv_factor(seg_ext, glu_ext, kernel)
    by_xy, probs, factor = lax.optimization_barrier((by_xy, probs, factor))
    w_conv_half = by_xy.transpose(1, 0, 2, 3).reshape(width, width // 2)

    conv_out_grad = pair_product(*halves(grad_out, core), w_conv_half)
    conv_grad = (conv_out_grad * factor).astype(jnp.bfloat16)
    grad_ext = padded(conv_grad, HALO)
    low_grad, high_grad, rows = conv_grads(seg_ext, grad_ext, glu_ext, pre_glu, kernel)
    low_own, low_away = halves(low_grad, core)
    high_own, high_away = halves(high_grad, core)

    rows = lax.all_to_all(
        rows.reshape(n_seq, (KW + 1) // n_seq, width), TIME, split_axis=0, concat_axis=0
    )
    rows = jnp.sum(rows, axis=0)

    gathered, rows = lax.optimization_barrier((gathered, rows))
    w_in_half = gathered[:, :width]
    w_attn = gathered[:, width:]
    norm_grad = pair_product(
        jnp.concatenate([low_own, high_own], axis=1),
        jnp.concatenate([low_away, high_away], axis=1),
        w_in_half,
    )
    inputs = saved_input.astype(jnp.float32)
    centred = inputs - jnp.mean(inputs, axis=1, keepdims=True)
    inv_std = 1.0 / jnp.sqrt(jnp.mean(centred * centred, axis=1, keepdims=True) + 1e-05)
    normed = centred * inv_std
    scaled_grad = norm_grad * norm_gain
    input_grad = inv_std * (
        scaled_grad
        - jnp.mean(scaled_grad, axis=1, keepdims=True)
        - normed * jnp.mean(scaled_grad * normed, axis=1, keepdims=True)
    )
    resid_grad = (grad_out.astype(jnp.float32) + input_grad).astype(jnp.bfloat16)
    ctx_t = jnp.einsum("rc,tc->rt", w_attn, resid_grad, preferred_element_type=jnp.float32)
    ctx_t = ctx_t.astype(jnp.bfloat16).reshape(n_seq, HD, t_dev)
    gain = jnp.sum(norm_grad * normed, axis=0, keepdims=True)
    ctx_t, gain = lax.optimization_barrier((ctx_t, gain))
    ctx_t = lax.all_to_all(ctx_t, TIME, split_axis=0, concat_axis=0)
    sums = jnp.concatenate([rows, gain], axis=0)
    for bit in (1, 2, 4):
        sums = sums + lax.ppermute(sums, "y", [(i, i ^ bit) for i in range(lax.axis_size("y"))])
    ctx_t, sums = lax.optimization_barrier((ctx_t, sums))
    probs = pltpu.with_memory_space_constraint(probs, pltpu.HBM)
    fixed = (bounds, probs, ctx_t, out_t, inv_sum, queries, keys.T, values)
    n = total // BLK
    stacked = spread(sums, "x")
    part_a, *acc = attention_grads(0, n // 2, *fixed)
    stacked, *acc = lax.optimization_barrier((stacked, *acc))
    sums = jnp.sum(stacked, axis=0)
    stacked = spread(sums, TIME)
    part_b, *acc = attention_grads(n // 2, n, *fixed, *acc)
    parts = [part_a, part_b]
    query_grad = jnp.concatenate(parts, axis=1).T
    key_grad, value_grad = [array.T for array in acc]
    kernel_grad = stacked[:, :-1].reshape(KW + 1, width)[:KW]
    gain_grad = jnp.sum(stacked[:, -1], axis=0)
    return (resid_grad, query_grad, key_grad, value_grad, kernel_grad, gain_grad)


def solution(mesh):
    dp, seq = mesh.devices.shape
    shape = (dp // 4, 4, seq // 2, 2)
    fine = Mesh(mesh.devices.reshape(shape), GROUPS + TIME)
    frames = P(GROUPS + TIME, None)
    heads = P(GROUPS, TIME)
    group = P(GROUPS, None)
    in_specs = (
        frames,
        frames,
        frames,
        heads,
        heads,
        heads,
        group,
        P(),
        P(),
        group,
        group,
        group,
    )
    out_specs = (frames, heads, heads, heads, P(), P())
    return jax.shard_map(local, mesh=fine, in_specs=in_specs, out_specs=out_specs, check_vma=False)
```

```python
import math

import jax
import jax.numpy as jnp
from jax import lax
from jax.experimental import pallas as pl
from jax.experimental.pallas import tpu as pltpu
from jax.sharding import Mesh
from jax.sharding import PartitionSpec as P

HD = 80
KW = 31
QBLK = 512
BLK = 256
HALO = 16
LANES = 128
TIME = ("z", "core")
GROUPS = ("far", "y", "x")


def frame_ends(frame_lens):
    n = frame_lens.shape[0]
    upto = jnp.arange(n)[:, None] >= jnp.arange(n)[None, :]
    return jnp.sum(jnp.where(upto, frame_lens[None, :], 0), axis=1).astype(jnp.int32)


def segments_of(ends, positions):
    counted = jnp.sum((positions[:, None] >= ends[None, :]).astype(jnp.int32), axis=1)
    return jnp.where(positions < 0, jnp.int32(-1), counted)


def padded(block, width):
    count = lax.axis_size(TIME)
    forward = [(i, i + 1) for i in range(count - 1)]
    backward = [(target, source) for source, target in forward]
    low = lax.ppermute(block[block.shape[0] - width :], TIME, forward)
    high = lax.ppermute(block[:width], TIME, backward)
    return jnp.concatenate([low, block, high], axis=0)


def spread(piece, axis):
    count = lax.axis_size(axis)
    copies = jnp.broadcast_to(piece[None], (count,) + piece.shape)
    return lax.all_to_all(copies, axis, split_axis=0, concat_axis=0)


def row_product(active, piece):
    return jnp.einsum("tc,rc->tr", active, piece, preferred_element_type=jnp.float32)


def halves(array, core):
    width = array.shape[1] // 2
    own = lax.dynamic_slice_in_dim(array, core * width, width, 1)
    away = lax.dynamic_slice_in_dim(array, (1 - core) * width, width, 1)
    return own, away


def swap(array):
    return lax.ppermute(array, "core", [(0, 1), (1, 0)])


def pair_product(own, away, piece):
    other = swap(away)
    back = swap(row_product(other, piece).astype(jnp.bfloat16))
    return row_product(own, piece) + back.astype(jnp.float32)


def fill_matches(seg, matches):
    rows = matches.shape[1]
    own = seg[pl.ds(HALO, rows), :]
    for tap in range(KW):
        there = seg[pl.ds(tap + HALO - KW // 2, rows), :]
        matches[tap] = jnp.where(there == own, 1.0, 0.0)


def conv_kernel(seg, glu, taps, factor, matches, wide):
    rows = factor.shape[0]

    @pl.when(pl.program_id(0) == 0)
    def _():
        fill_matches(seg, matches)

    wide[...] = glu[...].astype(jnp.float32)
    out = jnp.zeros(factor.shape, jnp.float32)
    for tap in range(KW):
        seen = wide[pl.ds(tap + HALO - KW // 2, rows), :] * matches[tap]
        out = out + taps[pl.ds(tap, 1), :] * seen
    sig = 1.0 / (1.0 + jnp.exp(-out))
    factor[...] = sig * (1.0 + out * (1.0 - sig))


def conv_factor(seg, glu_ext, taps):
    ext, width = glu_ext.shape
    rows = ext - 2 * HALO
    lanes = lambda count: pl.BlockSpec((count, LANES), lambda i: (0, i))
    return pl.pallas_call(
        conv_kernel,
        grid=(width // LANES,),
        in_specs=[pl.BlockSpec((ext, LANES), lambda i: (0, 0)), lanes(ext), lanes(KW)],
        out_specs=lanes(rows),
        out_shape=jax.ShapeDtypeStruct((rows, width), jnp.float32),
        scratch_shapes=[
            pltpu.VMEM((KW, rows, LANES), jnp.float32),
            pltpu.VMEM((ext, LANES), jnp.float32),
        ],
        compiler_params=pltpu.CompilerParams(vmem_limit_bytes=10 << 20),
        cost_estimate=pl.CostEstimate(
            flops=4 * KW * rows * width, transcendentals=rows * width, bytes_accessed=8 * rows * width
        ),
        name="conv_factor",
    )(seg, glu_ext, taps)


def conv_grads_kernel(
    seg, grad, glu, first_ref, gate_ref, taps, low, high, tap_grad, matches, wide_grad, wide_glu
):
    rows = low.shape[0]

    @pl.when(pl.program_id(0) == 0)
    def _():
        fill_matches(seg, matches)

    wide_grad[...] = grad[...].astype(jnp.float32)
    wide_glu[...] = glu[...].astype(jnp.float32)
    own = wide_grad[pl.ds(HALO, rows), :]
    glu_grad = jnp.zeros(low.shape, jnp.float32)
    for tap in range(KW):
        at = pl.ds(tap + HALO - KW // 2, rows)
        match = matches[tap]
        glu_grad = glu_grad + taps[pl.ds(KW - 1 - tap, 1), :] * (wide_grad[at, :] * match)
        tap_grad[pl.ds(tap, 1), :] = jnp.sum(own * (wide_glu[at, :] * match), axis=0, keepdims=True)
    tap_grad[pl.ds(KW, 1), :] = jnp.zeros((1, LANES), jnp.float32)
    first = first_ref[...].astype(jnp.float32)
    sig = 1.0 / (1.0 + jnp.exp(-gate_ref[...].astype(jnp.float32)))
    part = glu_grad * sig
    low[...] = part.astype(jnp.bfloat16)
    high[...] = (part * first * (1.0 - sig)).astype(jnp.bfloat16)


def conv_grads(seg, grad_ext, glu_ext, pre_glu, taps):
    ext, width = glu_ext.shape
    rows = ext - 2 * HALO
    n = width // LANES
    lanes = lambda count: pl.BlockSpec((count, LANES), lambda i: (0, i))
    return pl.pallas_call(
        conv_grads_kernel,
        grid=(n,),
        in_specs=[
            pl.BlockSpec((ext, LANES), lambda i: (0, 0)),
            lanes(ext),
            lanes(ext),
            lanes(rows),
            pl.BlockSpec((rows, LANES), lambda i: (0, i + n)),
            lanes(KW),
        ],
        out_specs=[lanes(rows), lanes(rows), lanes(KW + 1)],
        out_shape=[
            jax.ShapeDtypeStruct((rows, width), jnp.bfloat16),
            jax.ShapeDtypeStruct((rows, width), jnp.bfloat16),
            jax.ShapeDtypeStruct((KW + 1, width), jnp.float32),
        ],
        scratch_shapes=[
            pltpu.VMEM((KW, rows, LANES), jnp.float32),
            pltpu.VMEM((ext, LANES), jnp.float32),
            pltpu.VMEM((ext, LANES), jnp.float32),
        ],
        compiler_params=pltpu.CompilerParams(vmem_limit_bytes=10 << 20),
        cost_estimate=pl.CostEstimate(
            flops=8 * KW * rows * width, transcendentals=rows * width, bytes_accessed=16 * rows * width
        ),
        name="conv_grads",
    )(seg, grad_ext, glu_ext, pre_glu, pre_glu, taps)


def over_keys(first, last, step, carry):
    pairs = (last - first) // 2

    def pair(i, carry):
        return step(pl.multiple_of((first + 2 * i) * BLK, BLK), 2 * BLK, carry)

    def single(i, carry):
        return step(pl.multiple_of(i * BLK, BLK), BLK, carry)

    carry = lax.fori_loop(0, pairs, pair, carry)
    return lax.fori_loop(first + 2 * pairs, last, single, carry)


def probs_kernel(bounds, q_t, k, v_t, lo, hi, probs, out_t, inv_sum, scores):
    factor = math.log2(math.e) / math.sqrt(HD)
    block = pl.program_id(0)
    first = bounds[0, block]
    last = bounds[1, block]
    query = q_t[...]
    start = lo[...]
    end = hi[...]
    width = query.shape[1]

    def score(at, size, peak):
        rows = lax.broadcasted_iota(jnp.int32, (size, width), 0)
        s = jnp.dot(k[pl.ds(at, size), :], query, preferred_element_type=jnp.float32)
        valid = (rows >= start - at) & (rows < end - at)
        s = jnp.where(valid, s, -1e30)
        scores[pl.ds(at, size), :] = s
        return jnp.maximum(peak, jnp.max(s.reshape(size // 8, 8, width), axis=0))

    peak = over_keys(first, last, score, jnp.full((8, width), -1e30, jnp.float32))
    peak = jnp.max(peak, axis=0, keepdims=True)

    def expo(at, size, carry):
        total, acc = carry
        e = jnp.exp2((scores[pl.ds(at, size), :] - peak) * factor)
        low = e.astype(jnp.bfloat16)
        probs[pl.ds(at, size), :] = low
        acc = acc + jnp.dot(v_t[:, pl.ds(at, size)], low, preferred_element_type=jnp.float32)
        return total + jnp.sum(e.reshape(size // 8, 8, width), axis=0), acc

    total, acc = over_keys(
        first,
        last,
        expo,
        (jnp.zeros((8, width), jnp.float32), jnp.zeros((HD, width), jnp.float32)),
    )
    inv = 1.0 / jnp.sum(total, axis=0, keepdims=True)
    inv_sum[...] = inv
    out_t[...] = acc * inv


def attention_probs(bounds, q_t, keys, v_t, lo, hi):
    total = keys.shape[0]
    n = total // QBLK
    lanes = lambda rows: pl.BlockSpec((rows, QBLK), lambda i, b: (0, i))
    whole = lambda shape: pl.BlockSpec(shape, lambda i, b: (0, 0))
    return pl.pallas_call(
        probs_kernel,
        grid_spec=pltpu.PrefetchScalarGridSpec(
            num_scalar_prefetch=1,
            grid=(n,),
            in_specs=[
                lanes(HD),
                whole((total, HD)),
                whole((HD, total)),
                lanes(1),
                lanes(1),
            ],
            out_specs=[
                pl.BlockSpec((None, total, QBLK), lambda i, b: (i, 0, 0)),
                lanes(HD),
                lanes(1),
            ],
            scratch_shapes=[pltpu.VMEM((total, QBLK), jnp.float32)],
        ),
        out_shape=[
            pltpu.HBM((n, total, QBLK), jnp.bfloat16),
            jax.ShapeDtypeStruct((HD, total), jnp.float32),
            jax.ShapeDtypeStruct((1, total), jnp.float32),
        ],
        compiler_params=pltpu.CompilerParams(vmem_limit_bytes=20 << 20),
        cost_estimate=pl.CostEstimate(
            flops=2 * total * total * HD * 2,
            transcendentals=total * total // 2,
            bytes_accessed=total * total * 2,
        ),
        name="attention_probs",
    )(bounds, q_t, keys, v_t, lo, hi)


def grads_kernel(bounds, probs, ctx_t, out_t, inv_sum, q, k_t, v, dq_t, dk_t, dv_t, dk_acc, dv_acc):
    scale = 1.0 / math.sqrt(HD)
    block = pl.program_id(0)
    first = bounds[0, block]
    last = bounds[1, block]

    @pl.when(block == 0)
    def _():
        dk_acc[...] = jnp.zeros_like(dk_acc)
        dv_acc[...] = jnp.zeros_like(dv_acc)

    pieces = [ctx_t[i].astype(jnp.float32) for i in range(ctx_t.shape[0])]
    grad_t = jnp.concatenate(pieces, axis=1) * inv_sum[...]
    grad_low_t = grad_t.astype(jnp.bfloat16)
    grad_low = grad_t.T.astype(jnp.bfloat16)
    delta = jnp.sum(grad_low_t.astype(jnp.float32) * out_t[...], axis=0, keepdims=True)
    query = q[...]

    def step(at, size, acc):
        e = probs[pl.ds(at, size), :]
        prob_grad = jnp.dot(v[pl.ds(at, size), :], grad_low_t, preferred_element_type=jnp.float32)
        ds = (e.astype(jnp.float32) * (prob_grad - delta)).astype(jnp.bfloat16)
        dv_acc[pl.ds(at, size), :] += jnp.dot(e, grad_low, preferred_element_type=jnp.float32)
        dk_acc[pl.ds(at, size), :] += jnp.dot(ds, query, preferred_element_type=jnp.float32)
        return acc + jnp.dot(k_t[:, pl.ds(at, size)], ds, preferred_element_type=jnp.float32)

    acc = over_keys(first, last, step, jnp.zeros((HD, query.shape[0]), jnp.float32))
    dq_t[...] = (acc * scale).astype(jnp.bfloat16)

    @pl.when(block == pl.num_programs(0) - 1)
    def _():
        dk_t[...] = (dk_acc[...] * scale).T.astype(jnp.bfloat16)
        dv_t[...] = dv_acc[...].T.astype(jnp.bfloat16)


def attention_grads(bounds, probs, ctx_t, out_t, inv_sum, queries, k_t, values):
    total = queries.shape[0]
    n = total // QBLK
    per = QBLK // ctx_t.shape[2]
    lanes = lambda rows: pl.BlockSpec((rows, QBLK), lambda i, b: (0, i))
    whole = lambda shape: pl.BlockSpec(shape, lambda i, b: (0, 0))
    return pl.pallas_call(
        grads_kernel,
        grid_spec=pltpu.PrefetchScalarGridSpec(
            num_scalar_prefetch=1,
            grid=(n,),
            in_specs=[
                pl.BlockSpec((None, total, QBLK), lambda i, b: (i, 0, 0)),
                pl.BlockSpec((per, HD, ctx_t.shape[2]), lambda i, b: (i, 0, 0)),
                lanes(HD),
                lanes(1),
                pl.BlockSpec((QBLK, HD), lambda i, b: (i, 0)),
                whole((HD, total)),
                whole((total, HD)),
            ],
            out_specs=[lanes(HD), whole((HD, total)), whole((HD, total))],
            scratch_shapes=[pltpu.VMEM((total, HD), jnp.float32)] * 2,
        ),
        out_shape=[jax.ShapeDtypeStruct((HD, total), jnp.bfloat16)] * 3,
        compiler_params=pltpu.CompilerParams(vmem_limit_bytes=20 << 20),
        cost_estimate=pl.CostEstimate(
            flops=2 * total * total * HD * 4,
            transcendentals=0,
            bytes_accessed=total * total * 2,
        ),
        name="attention_grads",
    )(bounds, probs, ctx_t, out_t, inv_sum, queries, k_t, values)


def local(
    grad_out,
    saved_input,
    pre_glu,
    queries,
    keys,
    values,
    frame_counts,
    norm_gain,
    kernel,
    w_in,
    w_conv_out,
    w_attn_out,
):
    t_dev, width = grad_out.shape
    n_seq = lax.axis_size(TIME)
    total = t_dev * n_seq
    core = lax.axis_index("core")
    ends = frame_ends(frame_counts[0])

    in_low, _ = halves(w_in[:, :width], core)
    in_high, _ = halves(w_in[:, width:], core)
    gathered = lax.all_gather(
        jnp.concatenate([in_low, in_high, w_attn_out], axis=1), GROUPS, axis=0, tiled=True
    )

    positions = jnp.arange(total, dtype=jnp.int32)
    passed = positions[None, :] >= ends[:, None]
    lo = jnp.max(jnp.where(passed, ends[:, None], 0), axis=0, keepdims=True)
    hi = jnp.min(jnp.where(passed, total, ends[:, None]), axis=0, keepdims=True)
    bounds = jnp.stack([lo[0, ::QBLK] // BLK, (hi[0, QBLK - 1 :: QBLK] + BLK - 1) // BLK])

    conv_half, _ = halves(w_conv_out, core)
    by_y = spread(conv_half, ("far", "y"))
    ext_pos = lax.axis_index(TIME) * t_dev + jnp.arange(-HALO, t_dev + HALO, dtype=jnp.int32)
    seg_ext = jnp.broadcast_to(segments_of(ends, ext_pos)[:, None], (t_dev + 2 * HALO, LANES))
    gate_sig = jax.nn.sigmoid(pre_glu[:, width:].astype(jnp.float32))
    glu_out = (pre_glu[:, :width].astype(jnp.float32) * gate_sig).astype(jnp.bfloat16)
    glu_ext = padded(glu_out, HALO)
    by_y, lo = lax.optimization_barrier((by_y, lo))
    by_xy = spread(by_y, "x")
    probs, out_t, inv_sum = attention_probs(bounds, queries.T, keys, values.T, lo, hi)
    factor = conv_factor(seg_ext, glu_ext, kernel)
    by_xy, probs, factor = lax.optimization_barrier((by_xy, probs, factor))
    w_conv_half = by_xy.transpose(1, 0, 2, 3).reshape(width, width // 2)

    conv_out_grad = pair_product(*halves(grad_out, core), w_conv_half)
    conv_grad = (conv_out_grad * factor).astype(jnp.bfloat16)
    grad_ext = padded(conv_grad, HALO)
    low_grad, high_grad, rows = conv_grads(seg_ext, grad_ext, glu_ext, pre_glu, kernel)
    low_own, low_away = halves(low_grad, core)
    high_own, high_away = halves(high_grad, core)

    rows = lax.all_to_all(
        rows.reshape(n_seq, (KW + 1) // n_seq, width), TIME, split_axis=0, concat_axis=0
    )
    rows = jnp.sum(rows, axis=0)

    gathered, rows = lax.optimization_barrier((gathered, rows))
    w_in_half = gathered[:, :width]
    w_attn = gathered[:, width:]
    norm_grad = pair_product(
        jnp.concatenate([low_own, high_own], axis=1),
        jnp.concatenate([low_away, high_away], axis=1),
        w_in_half,
    )
    inputs = saved_input.astype(jnp.float32)
    centred = inputs - jnp.mean(inputs, axis=1, keepdims=True)
    inv_std = 1.0 / jnp.sqrt(jnp.mean(centred * centred, axis=1, keepdims=True) + 1e-05)
    normed = centred * inv_std
    scaled_grad = norm_grad * norm_gain
    input_grad = inv_std * (
        scaled_grad
        - jnp.mean(scaled_grad, axis=1, keepdims=True)
        - normed * jnp.mean(scaled_grad * normed, axis=1, keepdims=True)
    )
    resid_grad = (grad_out.astype(jnp.float32) + input_grad).astype(jnp.bfloat16)
    ctx_t = jnp.einsum("rc,tc->rt", w_attn, resid_grad, preferred_element_type=jnp.float32)
    ctx_t = ctx_t.astype(jnp.bfloat16).reshape(n_seq, HD, t_dev)
    gain = jnp.sum(norm_grad * normed, axis=0, keepdims=True)
    ctx_t, gain = lax.optimization_barrier((ctx_t, gain))
    ctx_t = lax.all_to_all(ctx_t, TIME, split_axis=0, concat_axis=0)
    sums = jnp.concatenate([rows, gain], axis=0)
    for bit in (1, 2):
        sums = sums + lax.ppermute(sums, "y", [(i, i ^ bit) for i in range(lax.axis_size("y"))])
    ctx_t, sums = lax.optimization_barrier((ctx_t, sums))
    probs = pltpu.with_memory_space_constraint(probs, pltpu.HBM)
    stacked = spread(sums, ("far", "x"))
    grads = attention_grads(bounds, probs, ctx_t, out_t, inv_sum, queries, keys.T, values)
    query_grad, key_grad, value_grad = [array.T for array in grads]
    stacked, query_grad = lax.optimization_barrier((stacked, query_grad))
    stacked = spread(jnp.sum(stacked, axis=0), TIME)
    kernel_grad = stacked[:, :-1].reshape(KW + 1, width)[:KW]
    gain_grad = jnp.sum(stacked[:, -1], axis=0)
    return (resid_grad, query_grad, key_grad, value_grad, kernel_grad, gain_grad)


def solution(mesh):
    dp, seq = mesh.devices.shape
    shape = (2, dp // 8, 4, seq // 2, 2)
    fine = Mesh(mesh.devices.reshape(shape), GROUPS + TIME)
    frames = P(GROUPS + TIME, None)
    heads = P(GROUPS, TIME)
    group = P(GROUPS, None)
    in_specs = (
        frames,
        frames,
        frames,
        heads,
        heads,
        heads,
        group,
        P(),
        P(),
        group,
        group,
        group,
    )
    out_specs = (frames, heads, heads, heads, P(), P())
    return jax.shard_map(local, mesh=fine, in_specs=in_specs, out_specs=out_specs, check_vma=False)
```

```python
import math

import jax
import jax.numpy as jnp
from jax import lax
from jax.experimental import pallas as pl
from jax.experimental.pallas import tpu as pltpu
from jax.sharding import Mesh
from jax.sharding import PartitionSpec as P

HD = 80
KW = 31
QBLK = 512
BLK = 256
HALO = 16
LANES = 128
TIME = ("z", "core")
GROUPS = ("far", "y", "x")


def frame_ends(frame_lens):
    n = frame_lens.shape[0]
    upto = jnp.arange(n)[:, None] >= jnp.arange(n)[None, :]
    return jnp.sum(jnp.where(upto, frame_lens[None, :], 0), axis=1).astype(jnp.int32)


def segments_of(ends, positions):
    counted = jnp.sum((positions[:, None] >= ends[None, :]).astype(jnp.int32), axis=1)
    return jnp.where(positions < 0, jnp.int32(-1), counted)


def padded(block, width):
    count = lax.axis_size(TIME)
    forward = [(i, i + 1) for i in range(count - 1)]
    backward = [(target, source) for source, target in forward]
    low = lax.ppermute(block[block.shape[0] - width :], TIME, forward)
    high = lax.ppermute(block[:width], TIME, backward)
    return jnp.concatenate([low, block, high], axis=0)


def spread(piece, axis):
    count = lax.axis_size(axis)
    copies = jnp.broadcast_to(piece[None], (count,) + piece.shape)
    return lax.all_to_all(copies, axis, split_axis=0, concat_axis=0)


def row_product(active, piece):
    return jnp.einsum("tc,rc->tr", active, piece, preferred_element_type=jnp.float32)


def halves(array, core):
    width = array.shape[1] // 2
    own = lax.dynamic_slice_in_dim(array, core * width, width, 1)
    away = lax.dynamic_slice_in_dim(array, (1 - core) * width, width, 1)
    return own, away


def swap(array):
    return lax.ppermute(array, "core", [(0, 1), (1, 0)])


def pair_product(own, away, piece):
    other = swap(away)
    back = swap(row_product(other, piece).astype(jnp.bfloat16))
    return row_product(own, piece) + back.astype(jnp.float32)


def fill_matches(seg, matches):
    rows = matches.shape[1]
    own = seg[pl.ds(HALO, rows), :]
    for tap in range(KW):
        there = seg[pl.ds(tap + HALO - KW // 2, rows), :]
        matches[tap] = jnp.where(there == own, 1.0, 0.0)


def conv_kernel(seg, glu, taps, factor, matches, wide):
    rows = factor.shape[0]

    @pl.when(pl.program_id(0) == 0)
    def _():
        fill_matches(seg, matches)

    wide[...] = glu[...].astype(jnp.float32)
    out = jnp.zeros(factor.shape, jnp.float32)
    for tap in range(KW):
        seen = wide[pl.ds(tap + HALO - KW // 2, rows), :] * matches[tap]
        out = out + taps[pl.ds(tap, 1), :] * seen
    sig = 1.0 / (1.0 + jnp.exp(-out))
    factor[...] = sig * (1.0 + out * (1.0 - sig))


def conv_factor(seg, glu_ext, taps):
    ext, width = glu_ext.shape
    rows = ext - 2 * HALO
    lanes = lambda count: pl.BlockSpec((count, LANES), lambda i: (0, i))
    return pl.pallas_call(
        conv_kernel,
        grid=(width // LANES,),
        in_specs=[pl.BlockSpec((ext, LANES), lambda i: (0, 0)), lanes(ext), lanes(KW)],
        out_specs=lanes(rows),
        out_shape=jax.ShapeDtypeStruct((rows, width), jnp.float32),
        scratch_shapes=[
            pltpu.VMEM((KW, rows, LANES), jnp.float32),
            pltpu.VMEM((ext, LANES), jnp.float32),
        ],
        compiler_params=pltpu.CompilerParams(vmem_limit_bytes=10 << 20),
        cost_estimate=pl.CostEstimate(
            flops=4 * KW * rows * width, transcendentals=rows * width, bytes_accessed=8 * rows * width
        ),
        name="conv_factor",
    )(seg, glu_ext, taps)


def conv_grads_kernel(
    seg, grad, glu, first_ref, gate_ref, taps, low, high, tap_grad, matches, wide_grad, wide_glu
):
    rows = low.shape[0]

    @pl.when(pl.program_id(0) == 0)
    def _():
        fill_matches(seg, matches)

    wide_grad[...] = grad[...].astype(jnp.float32)
    wide_glu[...] = glu[...].astype(jnp.float32)
    own = wide_grad[pl.ds(HALO, rows), :]
    glu_grad = jnp.zeros(low.shape, jnp.float32)
    for tap in range(KW):
        at = pl.ds(tap + HALO - KW // 2, rows)
        match = matches[tap]
        glu_grad = glu_grad + taps[pl.ds(KW - 1 - tap, 1), :] * (wide_grad[at, :] * match)
        tap_grad[pl.ds(tap, 1), :] = jnp.sum(own * (wide_glu[at, :] * match), axis=0, keepdims=True)
    tap_grad[pl.ds(KW, 1), :] = jnp.zeros((1, LANES), jnp.float32)
    first = first_ref[...].astype(jnp.float32)
    sig = 1.0 / (1.0 + jnp.exp(-gate_ref[...].astype(jnp.float32)))
    part = glu_grad * sig
    low[...] = part.astype(jnp.bfloat16)
    high[...] = (part * first * (1.0 - sig)).astype(jnp.bfloat16)


def conv_grads(seg, grad_ext, glu_ext, pre_glu, taps):
    ext, width = glu_ext.shape
    rows = ext - 2 * HALO
    n = width // LANES
    lanes = lambda count: pl.BlockSpec((count, LANES), lambda i: (0, i))
    return pl.pallas_call(
        conv_grads_kernel,
        grid=(n,),
        in_specs=[
            pl.BlockSpec((ext, LANES), lambda i: (0, 0)),
            lanes(ext),
            lanes(ext),
            lanes(rows),
            pl.BlockSpec((rows, LANES), lambda i: (0, i + n)),
            lanes(KW),
        ],
        out_specs=[lanes(rows), lanes(rows), lanes(KW + 1)],
        out_shape=[
            jax.ShapeDtypeStruct((rows, width), jnp.bfloat16),
            jax.ShapeDtypeStruct((rows, width), jnp.bfloat16),
            jax.ShapeDtypeStruct((KW + 1, width), jnp.float32),
        ],
        scratch_shapes=[
            pltpu.VMEM((KW, rows, LANES), jnp.float32),
            pltpu.VMEM((ext, LANES), jnp.float32),
            pltpu.VMEM((ext, LANES), jnp.float32),
        ],
        compiler_params=pltpu.CompilerParams(vmem_limit_bytes=10 << 20),
        cost_estimate=pl.CostEstimate(
            flops=8 * KW * rows * width, transcendentals=rows * width, bytes_accessed=16 * rows * width
        ),
        name="conv_grads",
    )(seg, grad_ext, glu_ext, pre_glu, pre_glu, taps)


def over_keys(first, last, step, carry):
    pairs = (last - first) // 2

    def pair(i, carry):
        return step(pl.multiple_of((first + 2 * i) * BLK, BLK), 2 * BLK, carry)

    def single(i, carry):
        return step(pl.multiple_of(i * BLK, BLK), BLK, carry)

    carry = lax.fori_loop(0, pairs, pair, carry)
    return lax.fori_loop(first + 2 * pairs, last, single, carry)


def probs_kernel(bounds, q_t, k, v_t, lo, hi, probs, out_t, inv_sum, scores):
    factor = math.log2(math.e) / math.sqrt(HD)
    block = pl.program_id(0)
    first = bounds[0, block]
    last = bounds[1, block]
    query = q_t[...]
    start = lo[...]
    end = hi[...]
    width = query.shape[1]

    def score(at, size, peak):
        rows = lax.broadcasted_iota(jnp.int32, (size, width), 0)
        s = jnp.dot(k[pl.ds(at, size), :], query, preferred_element_type=jnp.float32)
        valid = (rows >= start - at) & (rows < end - at)
        s = jnp.where(valid, s, -1e30)
        scores[pl.ds(at, size), :] = s
        return jnp.maximum(peak, jnp.max(s.reshape(size // 8, 8, width), axis=0))

    peak = over_keys(first, last, score, jnp.full((8, width), -1e30, jnp.float32))
    peak = jnp.max(peak, axis=0, keepdims=True)

    def expo(at, size, carry):
        total, acc = carry
        e = jnp.exp2((scores[pl.ds(at, size), :] - peak) * factor)
        low = e.astype(jnp.bfloat16)
        probs[pl.ds(at, size), :] = low
        acc = acc + jnp.dot(v_t[:, pl.ds(at, size)], low, preferred_element_type=jnp.float32)
        return total + jnp.sum(e.reshape(size // 8, 8, width), axis=0), acc

    total, acc = over_keys(
        first,
        last,
        expo,
        (jnp.zeros((8, width), jnp.float32), jnp.zeros((HD, width), jnp.float32)),
    )
    inv = 1.0 / jnp.sum(total, axis=0, keepdims=True)
    inv_sum[...] = inv
    out_t[...] = acc * inv


def attention_probs(bounds, q_t, keys, v_t, lo, hi):
    total = keys.shape[0]
    n = total // QBLK
    lanes = lambda rows: pl.BlockSpec((rows, QBLK), lambda i, b: (0, i))
    whole = lambda shape: pl.BlockSpec(shape, lambda i, b: (0, 0))
    return pl.pallas_call(
        probs_kernel,
        grid_spec=pltpu.PrefetchScalarGridSpec(
            num_scalar_prefetch=1,
            grid=(n,),
            in_specs=[
                lanes(HD),
                whole((total, HD)),
                whole((HD, total)),
                lanes(1),
                lanes(1),
            ],
            out_specs=[
                pl.BlockSpec((None, total, QBLK), lambda i, b: (i, 0, 0)),
                lanes(HD),
                lanes(1),
            ],
            scratch_shapes=[pltpu.VMEM((total, QBLK), jnp.float32)],
        ),
        out_shape=[
            pltpu.HBM((n, total, QBLK), jnp.bfloat16),
            jax.ShapeDtypeStruct((HD, total), jnp.float32),
            jax.ShapeDtypeStruct((1, total), jnp.float32),
        ],
        compiler_params=pltpu.CompilerParams(vmem_limit_bytes=20 << 20),
        cost_estimate=pl.CostEstimate(
            flops=2 * total * total * HD * 2,
            transcendentals=total * total // 2,
            bytes_accessed=total * total * 2,
        ),
        name="attention_probs",
    )(bounds, q_t, keys, v_t, lo, hi)


def grads_kernel(bounds, probs, ctx_t, out_t, inv_sum, q, k_t, v, dq_t, dk_t, dv_t, dk_acc, dv_acc):
    scale = 1.0 / math.sqrt(HD)
    block = pl.program_id(0)
    first = bounds[0, block]
    last = bounds[1, block]

    @pl.when(block == 0)
    def _():
        dk_acc[...] = jnp.zeros_like(dk_acc)
        dv_acc[...] = jnp.zeros_like(dv_acc)

    pieces = [ctx_t[i].astype(jnp.float32) for i in range(ctx_t.shape[0])]
    grad_t = jnp.concatenate(pieces, axis=1) * inv_sum[...]
    grad_low_t = grad_t.astype(jnp.bfloat16)
    grad_low = grad_t.T.astype(jnp.bfloat16)
    delta = jnp.sum(grad_low_t.astype(jnp.float32) * out_t[...], axis=0, keepdims=True)
    query = q[...]

    def step(at, size, acc):
        e = probs[pl.ds(at, size), :]
        prob_grad = jnp.dot(v[pl.ds(at, size), :], grad_low_t, preferred_element_type=jnp.float32)
        ds = (e.astype(jnp.float32) * (prob_grad - delta)).astype(jnp.bfloat16)
        dv_acc[pl.ds(at, size), :] += jnp.dot(e, grad_low, preferred_element_type=jnp.float32)
        dk_acc[pl.ds(at, size), :] += jnp.dot(ds, query, preferred_element_type=jnp.float32)
        return acc + jnp.dot(k_t[:, pl.ds(at, size)], ds, preferred_element_type=jnp.float32)

    acc = over_keys(first, last, step, jnp.zeros((HD, query.shape[0]), jnp.float32))
    dq_t[...] = (acc * scale).astype(jnp.bfloat16)

    @pl.when(block == pl.num_programs(0) - 1)
    def _():
        dk_t[...] = (dk_acc[...] * scale).T.astype(jnp.bfloat16)
        dv_t[...] = dv_acc[...].T.astype(jnp.bfloat16)


def attention_grads(bounds, probs, ctx_t, out_t, inv_sum, queries, k_t, values):
    total = queries.shape[0]
    n = total // QBLK
    per = QBLK // ctx_t.shape[2]
    lanes = lambda rows: pl.BlockSpec((rows, QBLK), lambda i, b: (0, i))
    whole = lambda shape: pl.BlockSpec(shape, lambda i, b: (0, 0))
    return pl.pallas_call(
        grads_kernel,
        grid_spec=pltpu.PrefetchScalarGridSpec(
            num_scalar_prefetch=1,
            grid=(n,),
            in_specs=[
                pl.BlockSpec((None, total, QBLK), lambda i, b: (i, 0, 0)),
                pl.BlockSpec((per, HD, ctx_t.shape[2]), lambda i, b: (i, 0, 0)),
                lanes(HD),
                lanes(1),
                pl.BlockSpec((QBLK, HD), lambda i, b: (i, 0)),
                whole((HD, total)),
                whole((total, HD)),
            ],
            out_specs=[lanes(HD), whole((HD, total)), whole((HD, total))],
            scratch_shapes=[pltpu.VMEM((total, HD), jnp.float32)] * 2,
        ),
        out_shape=[jax.ShapeDtypeStruct((HD, total), jnp.bfloat16)] * 3,
        compiler_params=pltpu.CompilerParams(vmem_limit_bytes=20 << 20),
        cost_estimate=pl.CostEstimate(
            flops=2 * total * total * HD * 4,
            transcendentals=0,
            bytes_accessed=total * total * 2,
        ),
        name="attention_grads",
    )(bounds, probs, ctx_t, out_t, inv_sum, queries, k_t, values)


def local(
    grad_out,
    saved_input,
    pre_glu,
    queries,
    keys,
    values,
    frame_counts,
    norm_gain,
    kernel,
    w_in,
    w_conv_out,
    w_attn_out,
):
    t_dev, width = grad_out.shape
    n_seq = lax.axis_size(TIME)
    total = t_dev * n_seq
    core = lax.axis_index("core")
    ends = frame_ends(frame_counts[0])

    in_low, _ = halves(w_in[:, :width], core)
    in_high, _ = halves(w_in[:, width:], core)
    gathered = lax.all_gather(
        jnp.concatenate([in_low, in_high, w_attn_out], axis=1), GROUPS, axis=0, tiled=True
    )

    positions = jnp.arange(total, dtype=jnp.int32)
    passed = positions[None, :] >= ends[:, None]
    lo = jnp.max(jnp.where(passed, ends[:, None], 0), axis=0, keepdims=True)
    hi = jnp.min(jnp.where(passed, total, ends[:, None]), axis=0, keepdims=True)
    bounds = jnp.stack([lo[0, ::QBLK] // BLK, (hi[0, QBLK - 1 :: QBLK] + BLK - 1) // BLK])

    conv_half, _ = halves(w_conv_out, core)
    by_y = spread(conv_half, ("far", "y"))
    ext_pos = lax.axis_index(TIME) * t_dev + jnp.arange(-HALO, t_dev + HALO, dtype=jnp.int32)
    seg_ext = jnp.broadcast_to(segments_of(ends, ext_pos)[:, None], (t_dev + 2 * HALO, LANES))
    gate_sig = jax.nn.sigmoid(pre_glu[:, width:].astype(jnp.float32))
    glu_out = (pre_glu[:, :width].astype(jnp.float32) * gate_sig).astype(jnp.bfloat16)
    glu_ext = padded(glu_out, HALO)
    by_y, lo = lax.optimization_barrier((by_y, lo))
    by_xy = spread(by_y, "x")
    probs, out_t, inv_sum = attention_probs(bounds, queries.T, keys, values.T, lo, hi)
    factor = conv_factor(seg_ext, glu_ext, kernel)
    by_xy, probs, factor = lax.optimization_barrier((by_xy, probs, factor))
    w_conv_half = by_xy.transpose(1, 0, 2, 3).reshape(width, width // 2)

    conv_out_grad = pair_product(*halves(grad_out, core), w_conv_half)
    conv_grad = (conv_out_grad * factor).astype(jnp.bfloat16)
    grad_ext = padded(conv_grad, HALO)
    low_grad, high_grad, rows = conv_grads(seg_ext, grad_ext, glu_ext, pre_glu, kernel)
    low_own, low_away = halves(low_grad, core)
    high_own, high_away = halves(high_grad, core)

    rows = rows.reshape(2, n_seq // 2, (KW + 1) // n_seq, width).transpose(1, 0, 2, 3)
    rows = rows.reshape(n_seq, (KW + 1) // n_seq, width)
    rows = jnp.sum(lax.all_to_all(rows, TIME, split_axis=0, concat_axis=0), axis=0)

    gathered, rows = lax.optimization_barrier((gathered, rows))
    w_in_half = gathered[:, :width]
    w_attn = gathered[:, width:]
    norm_grad = pair_product(
        jnp.concatenate([low_own, high_own], axis=1),
        jnp.concatenate([low_away, high_away], axis=1),
        w_in_half,
    )
    inputs = saved_input.astype(jnp.float32)
    centred = inputs - jnp.mean(inputs, axis=1, keepdims=True)
    inv_std = 1.0 / jnp.sqrt(jnp.mean(centred * centred, axis=1, keepdims=True) + 1e-05)
    normed = centred * inv_std
    scaled_grad = norm_grad * norm_gain
    input_grad = inv_std * (
        scaled_grad
        - jnp.mean(scaled_grad, axis=1, keepdims=True)
        - normed * jnp.mean(scaled_grad * normed, axis=1, keepdims=True)
    )
    resid_grad = (grad_out.astype(jnp.float32) + input_grad).astype(jnp.bfloat16)
    ctx_t = jnp.einsum("rc,tc->rt", w_attn, resid_grad, preferred_element_type=jnp.float32)
    ctx_t = ctx_t.astype(jnp.bfloat16).reshape(n_seq, HD, t_dev)
    gain = jnp.sum(norm_grad * normed, axis=0, keepdims=True)
    ctx_t, gain = lax.optimization_barrier((ctx_t, gain))
    ctx_t = lax.all_to_all(ctx_t, TIME, split_axis=0, concat_axis=0)
    sums = jnp.concatenate([rows, gain], axis=0)
    for axis in (("far", "y"), "x"):
        sums = jnp.sum(lax.all_gather(sums, axis), axis=0)
    ctx_t, sums = lax.optimization_barrier((ctx_t, sums))
    probs = pltpu.with_memory_space_constraint(probs, pltpu.HBM)
    stacked = spread(sums, "z")
    grads = attention_grads(bounds, probs, ctx_t, out_t, inv_sum, queries, keys.T, values)
    query_grad, key_grad, value_grad = [array.T for array in grads]
    stacked, query_grad = lax.optimization_barrier((stacked, query_grad))
    stacked = lax.all_gather(stacked, "core", axis=0)
    kernel_grad = stacked[:, :, :-1].reshape(KW + 1, width)[:KW]
    gain_grad = jnp.sum(stacked[:, :, -1], axis=(0, 1))
    return (resid_grad, query_grad, key_grad, value_grad, kernel_grad, gain_grad)


def solution(mesh):
    dp, seq = mesh.devices.shape
    shape = (2, dp // 8, 4, seq // 2, 2)
    fine = Mesh(mesh.devices.reshape(shape), GROUPS + TIME)
    frames = P(GROUPS + TIME, None)
    heads = P(GROUPS, TIME)
    group = P(GROUPS, None)
    in_specs = (
        frames,
        frames,
        frames,
        heads,
        heads,
        heads,
        group,
        P(),
        P(),
        group,
        group,
        group,
    )
    out_specs = (frames, heads, heads, heads, P(), P())
    return jax.shard_map(local, mesh=fine, in_specs=in_specs, out_specs=out_specs, check_vma=False)
```

```python
import math

import jax
import jax.numpy as jnp
from jax import lax
from jax.experimental import pallas as pl
from jax.experimental.pallas import tpu as pltpu
from jax.sharding import Mesh
from jax.sharding import PartitionSpec as P

HD = 80
KW = 31
QBLK = 512
BLK = 256
HALO = 16
LANES = 128
TIME = ("z", "core")
GROUPS = ("y", "x")


def frame_ends(frame_lens):
    n = frame_lens.shape[0]
    upto = jnp.arange(n)[:, None] >= jnp.arange(n)[None, :]
    return jnp.sum(jnp.where(upto, frame_lens[None, :], 0), axis=1).astype(jnp.int32)


def segments_of(ends, positions):
    counted = jnp.sum((positions[:, None] >= ends[None, :]).astype(jnp.int32), axis=1)
    return jnp.where(positions < 0, jnp.int32(-1), counted)


def padded(block, width):
    count = lax.axis_size(TIME)
    forward = [(i, i + 1) for i in range(count - 1)]
    backward = [(target, source) for source, target in forward]
    low = lax.ppermute(block[block.shape[0] - width :], TIME, forward)
    high = lax.ppermute(block[:width], TIME, backward)
    return jnp.concatenate([low, block, high], axis=0)


def spread(piece, axis):
    count = lax.axis_size(axis)
    copies = jnp.broadcast_to(piece[None], (count,) + piece.shape)
    return lax.all_to_all(copies, axis, split_axis=0, concat_axis=0)


def total_over(array, axis):
    count = lax.axis_size(axis)
    terms = [array]
    for bits in range(1, count):
        terms.append(lax.ppermute(array, axis, [(i, i ^ bits) for i in range(count)]))
    while len(terms) > 1:
        terms = [terms[i] + terms[i + 1] for i in range(0, len(terms), 2)]
    return terms[0]


def row_product(active, piece):
    return jnp.einsum("tc,rc->tr", active, piece, preferred_element_type=jnp.float32)


def halves(array, core):
    width = array.shape[1] // 2
    own = lax.dynamic_slice_in_dim(array, core * width, width, 1)
    away = lax.dynamic_slice_in_dim(array, (1 - core) * width, width, 1)
    return own, away


def swap(array):
    return lax.ppermute(array, "core", [(0, 1), (1, 0)])


def pair_product(own, away, piece):
    other = swap(away)
    back = swap(row_product(other, piece).astype(jnp.bfloat16))
    return row_product(own, piece) + back.astype(jnp.float32)


def fill_matches(seg, matches):
    rows = matches.shape[1]
    own = seg[pl.ds(HALO, rows), :]
    for tap in range(KW):
        there = seg[pl.ds(tap + HALO - KW // 2, rows), :]
        matches[tap] = jnp.where(there == own, 1.0, 0.0)


def conv_kernel(seg, glu, taps, factor, matches, wide):
    rows = factor.shape[0]

    @pl.when(pl.program_id(0) == 0)
    def _():
        fill_matches(seg, matches)

    wide[...] = glu[...].astype(jnp.float32)
    out = jnp.zeros(factor.shape, jnp.float32)
    for tap in range(KW):
        seen = wide[pl.ds(tap + HALO - KW // 2, rows), :] * matches[tap]
        out = out + taps[pl.ds(tap, 1), :] * seen
    sig = 1.0 / (1.0 + jnp.exp(-out))
    factor[...] = sig * (1.0 + out * (1.0 - sig))


def conv_factor(seg, glu_ext, taps):
    ext, width = glu_ext.shape
    rows = ext - 2 * HALO
    lanes = lambda count: pl.BlockSpec((count, LANES), lambda i: (0, i))
    return pl.pallas_call(
        conv_kernel,
        grid=(width // LANES,),
        in_specs=[pl.BlockSpec((ext, LANES), lambda i: (0, 0)), lanes(ext), lanes(KW)],
        out_specs=lanes(rows),
        out_shape=jax.ShapeDtypeStruct((rows, width), jnp.float32),
        scratch_shapes=[
            pltpu.VMEM((KW, rows, LANES), jnp.float32),
            pltpu.VMEM((ext, LANES), jnp.float32),
        ],
        compiler_params=pltpu.CompilerParams(vmem_limit_bytes=10 << 20),
        cost_estimate=pl.CostEstimate(
            flops=4 * KW * rows * width, transcendentals=rows * width, bytes_accessed=8 * rows * width
        ),
        name="conv_factor",
    )(seg, glu_ext, taps)


def conv_grads_kernel(
    seg, grad, glu, first_ref, gate_ref, taps, low, high, tap_grad, matches, wide_grad, wide_glu
):
    rows = low.shape[0]

    @pl.when(pl.program_id(0) == 0)
    def _():
        fill_matches(seg, matches)

    wide_grad[...] = grad[...].astype(jnp.float32)
    wide_glu[...] = glu[...].astype(jnp.float32)
    own = wide_grad[pl.ds(HALO, rows), :]
    glu_grad = jnp.zeros(low.shape, jnp.float32)
    for tap in range(KW):
        at = pl.ds(tap + HALO - KW // 2, rows)
        match = matches[tap]
        glu_grad = glu_grad + taps[pl.ds(KW - 1 - tap, 1), :] * (wide_grad[at, :] * match)
        tap_grad[pl.ds(tap, 1), :] = jnp.sum(own * (wide_glu[at, :] * match), axis=0, keepdims=True)
    tap_grad[pl.ds(KW, 1), :] = jnp.zeros((1, LANES), jnp.float32)
    first = first_ref[...].astype(jnp.float32)
    sig = 1.0 / (1.0 + jnp.exp(-gate_ref[...].astype(jnp.float32)))
    part = glu_grad * sig
    low[...] = part.astype(jnp.bfloat16)
    high[...] = (part * first * (1.0 - sig)).astype(jnp.bfloat16)


def conv_grads(seg, grad_ext, glu_ext, pre_glu, taps):
    ext, width = glu_ext.shape
    rows = ext - 2 * HALO
    n = width // LANES
    lanes = lambda count: pl.BlockSpec((count, LANES), lambda i: (0, i))
    return pl.pallas_call(
        conv_grads_kernel,
        grid=(n,),
        in_specs=[
            pl.BlockSpec((ext, LANES), lambda i: (0, 0)),
            lanes(ext),
            lanes(ext),
            lanes(rows),
            pl.BlockSpec((rows, LANES), lambda i: (0, i + n)),
            lanes(KW),
        ],
        out_specs=[lanes(rows), lanes(rows), lanes(KW + 1)],
        out_shape=[
            jax.ShapeDtypeStruct((rows, width), jnp.bfloat16),
            jax.ShapeDtypeStruct((rows, width), jnp.bfloat16),
            jax.ShapeDtypeStruct((KW + 1, width), jnp.float32),
        ],
        scratch_shapes=[
            pltpu.VMEM((KW, rows, LANES), jnp.float32),
            pltpu.VMEM((ext, LANES), jnp.float32),
            pltpu.VMEM((ext, LANES), jnp.float32),
        ],
        compiler_params=pltpu.CompilerParams(vmem_limit_bytes=10 << 20),
        cost_estimate=pl.CostEstimate(
            flops=8 * KW * rows * width, transcendentals=rows * width, bytes_accessed=16 * rows * width
        ),
        name="conv_grads",
    )(seg, grad_ext, glu_ext, pre_glu, pre_glu, taps)


def over_keys(first, last, step, carry):
    pairs = (last - first) // 2

    def pair(i, carry):
        return step(pl.multiple_of((first + 2 * i) * BLK, BLK), 2 * BLK, carry)

    def single(i, carry):
        return step(pl.multiple_of(i * BLK, BLK), BLK, carry)

    carry = lax.fori_loop(0, pairs, pair, carry)
    return lax.fori_loop(first + 2 * pairs, last, single, carry)


def probs_kernel(bounds, q_t, k, v_t, lo, hi, probs, out_t, inv_sum, scores):
    factor = math.log2(math.e) / math.sqrt(HD)
    block = pl.program_id(0)
    first = bounds[0, block]
    last = bounds[1, block]
    query = q_t[...]
    start = lo[...]
    end = hi[...]
    width = query.shape[1]

    def score(at, size, peak):
        rows = lax.broadcasted_iota(jnp.int32, (size, width), 0)
        s = jnp.dot(k[pl.ds(at, size), :], query, preferred_element_type=jnp.float32)
        valid = (rows >= start - at) & (rows < end - at)
        s = jnp.where(valid, s, -1e30)
        scores[pl.ds(at, size), :] = s
        return jnp.maximum(peak, jnp.max(s.reshape(size // 8, 8, width), axis=0))

    peak = over_keys(first, last, score, jnp.full((8, width), -1e30, jnp.float32))
    peak = jnp.max(peak, axis=0, keepdims=True)

    def expo(at, size, carry):
        total, acc = carry
        e = jnp.exp2((scores[pl.ds(at, size), :] - peak) * factor)
        low = e.astype(jnp.bfloat16)
        probs[pl.ds(at, size), :] = low
        acc = acc + jnp.dot(v_t[:, pl.ds(at, size)], low, preferred_element_type=jnp.float32)
        return total + jnp.sum(e.reshape(size // 8, 8, width), axis=0), acc

    total, acc = over_keys(
        first,
        last,
        expo,
        (jnp.zeros((8, width), jnp.float32), jnp.zeros((HD, width), jnp.float32)),
    )
    inv = 1.0 / jnp.sum(total, axis=0, keepdims=True)
    inv_sum[...] = inv
    out_t[...] = acc * inv


def attention_probs(bounds, q_t, keys, v_t, lo, hi):
    total = keys.shape[0]
    n = total // QBLK
    lanes = lambda rows: pl.BlockSpec((rows, QBLK), lambda i, b: (0, i))
    whole = lambda shape: pl.BlockSpec(shape, lambda i, b: (0, 0))
    return pl.pallas_call(
        probs_kernel,
        grid_spec=pltpu.PrefetchScalarGridSpec(
            num_scalar_prefetch=1,
            grid=(n,),
            in_specs=[
                lanes(HD),
                whole((total, HD)),
                whole((HD, total)),
                lanes(1),
                lanes(1),
            ],
            out_specs=[
                pl.BlockSpec((None, total, QBLK), lambda i, b: (i, 0, 0)),
                lanes(HD),
                lanes(1),
            ],
            scratch_shapes=[pltpu.VMEM((total, QBLK), jnp.float32)],
        ),
        out_shape=[
            pltpu.HBM((n, total, QBLK), jnp.bfloat16),
            jax.ShapeDtypeStruct((HD, total), jnp.float32),
            jax.ShapeDtypeStruct((1, total), jnp.float32),
        ],
        compiler_params=pltpu.CompilerParams(vmem_limit_bytes=20 << 20),
        cost_estimate=pl.CostEstimate(
            flops=2 * total * total * HD * 2,
            transcendentals=total * total // 2,
            bytes_accessed=total * total * 2,
        ),
        name="attention_probs",
    )(bounds, q_t, keys, v_t, lo, hi)


def grads_kernel(bounds, probs, ctx_t, out_t, inv_sum, q, k_t, v, dq_t, dk_t, dv_t, dk_acc, dv_acc):
    scale = 1.0 / math.sqrt(HD)
    block = pl.program_id(0)
    first = bounds[0, block]
    last = bounds[1, block]

    @pl.when(block == 0)
    def _():
        dk_acc[...] = jnp.zeros_like(dk_acc)
        dv_acc[...] = jnp.zeros_like(dv_acc)

    pieces = [ctx_t[i].astype(jnp.float32) for i in range(ctx_t.shape[0])]
    grad_t = jnp.concatenate(pieces, axis=1) * inv_sum[...]
    grad_low_t = grad_t.astype(jnp.bfloat16)
    grad_low = grad_t.T.astype(jnp.bfloat16)
    delta = jnp.sum(grad_low_t.astype(jnp.float32) * out_t[...], axis=0, keepdims=True)
    query = q[...]

    def step(at, size, acc):
        e = probs[pl.ds(at, size), :]
        prob_grad = jnp.dot(v[pl.ds(at, size), :], grad_low_t, preferred_element_type=jnp.float32)
        ds = (e.astype(jnp.float32) * (prob_grad - delta)).astype(jnp.bfloat16)
        dv_acc[pl.ds(at, size), :] += jnp.dot(e, grad_low, preferred_element_type=jnp.float32)
        dk_acc[pl.ds(at, size), :] += jnp.dot(ds, query, preferred_element_type=jnp.float32)
        return acc + jnp.dot(k_t[:, pl.ds(at, size)], ds, preferred_element_type=jnp.float32)

    acc = over_keys(first, last, step, jnp.zeros((HD, query.shape[0]), jnp.float32))
    dq_t[...] = (acc * scale).astype(jnp.bfloat16)

    @pl.when(block == pl.num_programs(0) - 1)
    def _():
        dk_t[...] = (dk_acc[...] * scale).T.astype(jnp.bfloat16)
        dv_t[...] = dv_acc[...].T.astype(jnp.bfloat16)


def attention_grads(bounds, probs, ctx_t, out_t, inv_sum, queries, k_t, values):
    total = queries.shape[0]
    n = total // QBLK
    per = QBLK // ctx_t.shape[2]
    lanes = lambda rows: pl.BlockSpec((rows, QBLK), lambda i, b: (0, i))
    whole = lambda shape: pl.BlockSpec(shape, lambda i, b: (0, 0))
    return pl.pallas_call(
        grads_kernel,
        grid_spec=pltpu.PrefetchScalarGridSpec(
            num_scalar_prefetch=1,
            grid=(n,),
            in_specs=[
                pl.BlockSpec((None, total, QBLK), lambda i, b: (i, 0, 0)),
                pl.BlockSpec((per, HD, ctx_t.shape[2]), lambda i, b: (i, 0, 0)),
                lanes(HD),
                lanes(1),
                pl.BlockSpec((QBLK, HD), lambda i, b: (i, 0)),
                whole((HD, total)),
                whole((total, HD)),
            ],
            out_specs=[lanes(HD), whole((HD, total)), whole((HD, total))],
            scratch_shapes=[pltpu.VMEM((total, HD), jnp.float32)] * 2,
        ),
        out_shape=[jax.ShapeDtypeStruct((HD, total), jnp.bfloat16)] * 3,
        compiler_params=pltpu.CompilerParams(vmem_limit_bytes=20 << 20),
        cost_estimate=pl.CostEstimate(
            flops=2 * total * total * HD * 4,
            transcendentals=0,
            bytes_accessed=total * total * 2,
        ),
        name="attention_grads",
    )(bounds, probs, ctx_t, out_t, inv_sum, queries, k_t, values)


def local(
    grad_out,
    saved_input,
    pre_glu,
    queries,
    keys,
    values,
    frame_counts,
    norm_gain,
    kernel,
    w_in,
    w_conv_out,
    w_attn_out,
):
    t_dev, width = grad_out.shape
    n_seq = lax.axis_size(TIME)
    total = t_dev * n_seq
    core = lax.axis_index("core")
    ends = frame_ends(frame_counts[0])

    in_low, _ = halves(w_in[:, :width], core)
    in_high, _ = halves(w_in[:, width:], core)
    gathered = lax.all_gather(
        jnp.concatenate([in_low, in_high, w_attn_out], axis=1), GROUPS, axis=0, tiled=True
    )

    positions = jnp.arange(total, dtype=jnp.int32)
    passed = positions[None, :] >= ends[:, None]
    lo = jnp.max(jnp.where(passed, ends[:, None], 0), axis=0, keepdims=True)
    hi = jnp.min(jnp.where(passed, total, ends[:, None]), axis=0, keepdims=True)
    bounds = jnp.stack([lo[0, ::QBLK] // BLK, (hi[0, QBLK - 1 :: QBLK] + BLK - 1) // BLK])

    conv_half, _ = halves(w_conv_out, core)
    by_y = spread(conv_half, "y")
    ext_pos = lax.axis_index(TIME) * t_dev + jnp.arange(-HALO, t_dev + HALO, dtype=jnp.int32)
    seg_ext = jnp.broadcast_to(segments_of(ends, ext_pos)[:, None], (t_dev + 2 * HALO, LANES))
    gate_sig = jax.nn.sigmoid(pre_glu[:, width:].astype(jnp.float32))
    glu_out = (pre_glu[:, :width].astype(jnp.float32) * gate_sig).astype(jnp.bfloat16)
    glu_ext = padded(glu_out, HALO)
    by_y, lo = lax.optimization_barrier((by_y, lo))
    by_xy = spread(by_y, "x")
    probs, out_t, inv_sum = attention_probs(bounds, queries.T, keys, values.T, lo, hi)
    factor = conv_factor(seg_ext, glu_ext, kernel)
    by_xy, probs, factor = lax.optimization_barrier((by_xy, probs, factor))
    w_conv_half = by_xy.transpose(1, 0, 2, 3).reshape(width, width // 2)

    conv_out_grad = pair_product(*halves(grad_out, core), w_conv_half)
    conv_grad = (conv_out_grad * factor).astype(jnp.bfloat16)
    grad_ext = padded(conv_grad, HALO)
    low_grad, high_grad, rows = conv_grads(seg_ext, grad_ext, glu_ext, pre_glu, kernel)
    low_own, low_away = halves(low_grad, core)
    high_own, high_away = halves(high_grad, core)

    rows = rows.reshape(2, n_seq // 2, (KW + 1) // n_seq, width).transpose(1, 0, 2, 3)
    rows = rows.reshape(n_seq, (KW + 1) // n_seq, width)
    rows = jnp.sum(lax.all_to_all(rows, TIME, split_axis=0, concat_axis=0), axis=0)

    gathered, rows = lax.optimization_barrier((gathered, rows))
    w_in_half = gathered[:, :width]
    w_attn = gathered[:, width:]
    norm_grad = pair_product(
        jnp.concatenate([low_own, high_own], axis=1),
        jnp.concatenate([low_away, high_away], axis=1),
        w_in_half,
    )
    inputs = saved_input.astype(jnp.float32)
    centred = inputs - jnp.mean(inputs, axis=1, keepdims=True)
    inv_std = 1.0 / jnp.sqrt(jnp.mean(centred * centred, axis=1, keepdims=True) + 1e-05)
    normed = centred * inv_std
    scaled_grad = norm_grad * norm_gain
    input_grad = inv_std * (
        scaled_grad
        - jnp.mean(scaled_grad, axis=1, keepdims=True)
        - normed * jnp.mean(scaled_grad * normed, axis=1, keepdims=True)
    )
    resid_grad = (grad_out.astype(jnp.float32) + input_grad).astype(jnp.bfloat16)
    ctx_t = jnp.einsum("rc,tc->rt", w_attn, resid_grad, preferred_element_type=jnp.float32)
    ctx_t = ctx_t.astype(jnp.bfloat16).reshape(n_seq, HD, t_dev)
    gain = jnp.sum(norm_grad * normed, axis=0, keepdims=True)
    ctx_t, gain = lax.optimization_barrier((ctx_t, gain))
    ctx_t = lax.all_to_all(ctx_t, TIME, split_axis=0, concat_axis=0)
    sums = jnp.concatenate([rows, gain], axis=0)
    for axis in ("x", "y"):
        sums = total_over(sums, axis)
    ctx_t, sums = lax.optimization_barrier((ctx_t, sums))
    probs = pltpu.with_memory_space_constraint(probs, pltpu.HBM)
    stacked = spread(sums, "z")
    grads = attention_grads(bounds, probs, ctx_t, out_t, inv_sum, queries, keys.T, values)
    query_grad, key_grad, value_grad = [array.T for array in grads]
    stacked, query_grad = lax.optimization_barrier((stacked, query_grad))
    stacked = lax.all_gather(stacked, "core", axis=0)
    kernel_grad = stacked[:, :, :-1].reshape(KW + 1, width)[:KW]
    gain_grad = jnp.sum(stacked[:, :, -1], axis=(0, 1))
    return (resid_grad, query_grad, key_grad, value_grad, kernel_grad, gain_grad)


def solution(mesh):
    dp, seq = mesh.devices.shape
    shape = (dp // 4, 4, seq // 2, 2)
    fine = Mesh(mesh.devices.reshape(shape), GROUPS + TIME)
    frames = P(GROUPS + TIME, None)
    heads = P(GROUPS, TIME)
    group = P(GROUPS, None)
    in_specs = (
        frames,
        frames,
        frames,
        heads,
        heads,
        heads,
        group,
        P(),
        P(),
        group,
        group,
        group,
    )
    out_specs = (frames, heads, heads, heads, P(), P())
    return jax.shard_map(local, mesh=fine, in_specs=in_specs, out_specs=out_specs, check_vma=False)
```

```python
import math

import jax
import jax.numpy as jnp
from jax import lax
from jax.experimental import pallas as pl
from jax.experimental.pallas import tpu as pltpu
from jax.sharding import Mesh
from jax.sharding import PartitionSpec as P

HD = 80
KW = 31
QBLK = 512
BLK = 256
HALO = 16
LANES = 128
TIME = ("z", "core")
GROUPS = ("far", "y", "x")


def frame_ends(frame_lens):
    n = frame_lens.shape[0]
    upto = jnp.arange(n)[:, None] >= jnp.arange(n)[None, :]
    return jnp.sum(jnp.where(upto, frame_lens[None, :], 0), axis=1).astype(jnp.int32)


def segments_of(ends, positions):
    counted = jnp.sum((positions[:, None] >= ends[None, :]).astype(jnp.int32), axis=1)
    return jnp.where(positions < 0, jnp.int32(-1), counted)


def padded(block, width):
    count = lax.axis_size(TIME)
    forward = [(i, i + 1) for i in range(count - 1)]
    backward = [(target, source) for source, target in forward]
    low = lax.ppermute(block[block.shape[0] - width :], TIME, forward)
    high = lax.ppermute(block[:width], TIME, backward)
    return jnp.concatenate([low, block, high], axis=0)


def spread(piece, axis):
    count = lax.axis_size(axis)
    copies = jnp.broadcast_to(piece[None], (count,) + piece.shape)
    return lax.all_to_all(copies, axis, split_axis=0, concat_axis=0)


def row_product(active, piece):
    return jnp.einsum("tc,rc->tr", active, piece, preferred_element_type=jnp.float32)


def halves(array, core):
    width = array.shape[1] // 2
    own = lax.dynamic_slice_in_dim(array, core * width, width, 1)
    away = lax.dynamic_slice_in_dim(array, (1 - core) * width, width, 1)
    return own, away


def swap(array):
    return lax.ppermute(array, "core", [(0, 1), (1, 0)])


def pair_product(own, away, piece):
    other = swap(away)
    back = swap(row_product(other, piece).astype(jnp.bfloat16))
    return row_product(own, piece) + back.astype(jnp.float32)


def fill_matches(seg, matches):
    rows = matches.shape[1]
    own = seg[pl.ds(HALO, rows), :]
    for tap in range(KW):
        there = seg[pl.ds(tap + HALO - KW // 2, rows), :]
        matches[tap] = jnp.where(there == own, 1.0, 0.0)


def conv_kernel(seg, glu, taps, factor, matches, wide):
    rows = factor.shape[0]

    @pl.when(pl.program_id(0) == 0)
    def _():
        fill_matches(seg, matches)

    wide[...] = glu[...].astype(jnp.float32)
    out = jnp.zeros(factor.shape, jnp.float32)
    for tap in range(KW):
        seen = wide[pl.ds(tap + HALO - KW // 2, rows), :] * matches[tap]
        out = out + taps[pl.ds(tap, 1), :] * seen
    sig = 1.0 / (1.0 + jnp.exp(-out))
    factor[...] = sig * (1.0 + out * (1.0 - sig))


def conv_factor(seg, glu_ext, taps):
    ext, width = glu_ext.shape
    rows = ext - 2 * HALO
    lanes = lambda count: pl.BlockSpec((count, LANES), lambda i: (0, i))
    return pl.pallas_call(
        conv_kernel,
        grid=(width // LANES,),
        in_specs=[pl.BlockSpec((ext, LANES), lambda i: (0, 0)), lanes(ext), lanes(KW)],
        out_specs=lanes(rows),
        out_shape=jax.ShapeDtypeStruct((rows, width), jnp.float32),
        scratch_shapes=[
            pltpu.VMEM((KW, rows, LANES), jnp.float32),
            pltpu.VMEM((ext, LANES), jnp.float32),
        ],
        compiler_params=pltpu.CompilerParams(vmem_limit_bytes=10 << 20),
        cost_estimate=pl.CostEstimate(
            flops=4 * KW * rows * width, transcendentals=rows * width, bytes_accessed=8 * rows * width
        ),
        name="conv_factor",
    )(seg, glu_ext, taps)


def conv_grads_kernel(
    seg, grad, glu, first_ref, gate_ref, taps, low, high, tap_grad, matches, wide_grad, wide_glu
):
    rows = low.shape[0]

    @pl.when(pl.program_id(0) == 0)
    def _():
        fill_matches(seg, matches)

    wide_grad[...] = grad[...].astype(jnp.float32)
    wide_glu[...] = glu[...].astype(jnp.float32)
    own = wide_grad[pl.ds(HALO, rows), :]
    glu_grad = jnp.zeros(low.shape, jnp.float32)
    for tap in range(KW):
        at = pl.ds(tap + HALO - KW // 2, rows)
        match = matches[tap]
        glu_grad = glu_grad + taps[pl.ds(KW - 1 - tap, 1), :] * (wide_grad[at, :] * match)
        tap_grad[pl.ds(tap, 1), :] = jnp.sum(own * (wide_glu[at, :] * match), axis=0, keepdims=True)
    tap_grad[pl.ds(KW, 1), :] = jnp.zeros((1, LANES), jnp.float32)
    first = first_ref[...].astype(jnp.float32)
    sig = 1.0 / (1.0 + jnp.exp(-gate_ref[...].astype(jnp.float32)))
    part = glu_grad * sig
    low[...] = part.astype(jnp.bfloat16)
    high[...] = (part * first * (1.0 - sig)).astype(jnp.bfloat16)


def conv_grads(seg, grad_ext, glu_ext, pre_glu, taps):
    ext, width = glu_ext.shape
    rows = ext - 2 * HALO
    n = width // LANES
    lanes = lambda count: pl.BlockSpec((count, LANES), lambda i: (0, i))
    return pl.pallas_call(
        conv_grads_kernel,
        grid=(n,),
        in_specs=[
            pl.BlockSpec((ext, LANES), lambda i: (0, 0)),
            lanes(ext),
            lanes(ext),
            lanes(rows),
            pl.BlockSpec((rows, LANES), lambda i: (0, i + n)),
            lanes(KW),
        ],
        out_specs=[lanes(rows), lanes(rows), lanes(KW + 1)],
        out_shape=[
            jax.ShapeDtypeStruct((rows, width), jnp.bfloat16),
            jax.ShapeDtypeStruct((rows, width), jnp.bfloat16),
            jax.ShapeDtypeStruct((KW + 1, width), jnp.float32),
        ],
        scratch_shapes=[
            pltpu.VMEM((KW, rows, LANES), jnp.float32),
            pltpu.VMEM((ext, LANES), jnp.float32),
            pltpu.VMEM((ext, LANES), jnp.float32),
        ],
        compiler_params=pltpu.CompilerParams(vmem_limit_bytes=10 << 20),
        cost_estimate=pl.CostEstimate(
            flops=8 * KW * rows * width, transcendentals=rows * width, bytes_accessed=16 * rows * width
        ),
        name="conv_grads",
    )(seg, grad_ext, glu_ext, pre_glu, pre_glu, taps)


def over_keys(first, last, step, carry):
    pairs = (last - first) // 2

    def pair(i, carry):
        return step(pl.multiple_of((first + 2 * i) * BLK, BLK), 2 * BLK, carry)

    def single(i, carry):
        return step(pl.multiple_of(i * BLK, BLK), BLK, carry)

    carry = lax.fori_loop(0, pairs, pair, carry)
    return lax.fori_loop(first + 2 * pairs, last, single, carry)


def probs_kernel(bounds, q_t, k, v_t, lo, hi, probs, out_t, inv_sum, scores):
    factor = math.log2(math.e) / math.sqrt(HD)
    block = pl.program_id(0)
    first = bounds[0, block]
    last = bounds[1, block]
    query = q_t[...]
    start = lo[...]
    end = hi[...]
    width = query.shape[1]

    def score(at, size, peak):
        rows = lax.broadcasted_iota(jnp.int32, (size, width), 0)
        s = jnp.dot(k[pl.ds(at, size), :], query, preferred_element_type=jnp.float32)
        valid = (rows >= start - at) & (rows < end - at)
        s = jnp.where(valid, s, -1e30)
        scores[pl.ds(at, size), :] = s
        return jnp.maximum(peak, jnp.max(s.reshape(size // 8, 8, width), axis=0))

    peak = over_keys(first, last, score, jnp.full((8, width), -1e30, jnp.float32))
    peak = jnp.max(peak, axis=0, keepdims=True)

    def expo(at, size, carry):
        total, acc = carry
        e = jnp.exp2((scores[pl.ds(at, size), :] - peak) * factor)
        low = e.astype(jnp.bfloat16)
        probs[pl.ds(at, size), :] = low
        acc = acc + jnp.dot(v_t[:, pl.ds(at, size)], low, preferred_element_type=jnp.float32)
        return total + jnp.sum(e.reshape(size // 8, 8, width), axis=0), acc

    total, acc = over_keys(
        first,
        last,
        expo,
        (jnp.zeros((8, width), jnp.float32), jnp.zeros((HD, width), jnp.float32)),
    )
    inv = 1.0 / jnp.sum(total, axis=0, keepdims=True)
    inv_sum[...] = inv
    out_t[...] = acc * inv


def attention_probs(bounds, q_t, keys, v_t, lo, hi):
    total = keys.shape[0]
    n = total // QBLK
    lanes = lambda rows: pl.BlockSpec((rows, QBLK), lambda i, b: (0, i))
    whole = lambda shape: pl.BlockSpec(shape, lambda i, b: (0, 0))
    return pl.pallas_call(
        probs_kernel,
        grid_spec=pltpu.PrefetchScalarGridSpec(
            num_scalar_prefetch=1,
            grid=(n,),
            in_specs=[
                lanes(HD),
                whole((total, HD)),
                whole((HD, total)),
                lanes(1),
                lanes(1),
            ],
            out_specs=[
                pl.BlockSpec((None, total, QBLK), lambda i, b: (i, 0, 0)),
                lanes(HD),
                lanes(1),
            ],
            scratch_shapes=[pltpu.VMEM((total, QBLK), jnp.float32)],
        ),
        out_shape=[
            pltpu.HBM((n, total, QBLK), jnp.bfloat16),
            jax.ShapeDtypeStruct((HD, total), jnp.float32),
            jax.ShapeDtypeStruct((1, total), jnp.float32),
        ],
        compiler_params=pltpu.CompilerParams(vmem_limit_bytes=20 << 20),
        cost_estimate=pl.CostEstimate(
            flops=2 * total * total * HD * 2,
            transcendentals=total * total // 2,
            bytes_accessed=total * total * 2,
        ),
        name="attention_probs",
    )(bounds, q_t, keys, v_t, lo, hi)


def grads_kernel(bounds, probs, ctx_t, out_t, inv_sum, q, k_t, v, dq_t, dk_t, dv_t, dk_acc, dv_acc):
    scale = 1.0 / math.sqrt(HD)
    block = pl.program_id(0)
    first = bounds[0, block]
    last = bounds[1, block]

    @pl.when(block == 0)
    def _():
        dk_acc[...] = jnp.zeros_like(dk_acc)
        dv_acc[...] = jnp.zeros_like(dv_acc)

    pieces = [ctx_t[i].astype(jnp.float32) for i in range(ctx_t.shape[0])]
    grad_t = jnp.concatenate(pieces, axis=1) * inv_sum[...]
    grad_low_t = grad_t.astype(jnp.bfloat16)
    grad_low = grad_t.T.astype(jnp.bfloat16)
    delta = jnp.sum(grad_low_t.astype(jnp.float32) * out_t[...], axis=0, keepdims=True)
    query = q[...]

    def step(at, size, acc):
        e = probs[pl.ds(at, size), :]
        prob_grad = jnp.dot(v[pl.ds(at, size), :], grad_low_t, preferred_element_type=jnp.float32)
        ds = (e.astype(jnp.float32) * (prob_grad - delta)).astype(jnp.bfloat16)
        dv_acc[pl.ds(at, size), :] += jnp.dot(e, grad_low, preferred_element_type=jnp.float32)
        dk_acc[pl.ds(at, size), :] += jnp.dot(ds, query, preferred_element_type=jnp.float32)
        return acc + jnp.dot(k_t[:, pl.ds(at, size)], ds, preferred_element_type=jnp.float32)

    acc = over_keys(first, last, step, jnp.zeros((HD, query.shape[0]), jnp.float32))
    dq_t[...] = (acc * scale).astype(jnp.bfloat16)

    @pl.when(block == pl.num_programs(0) - 1)
    def _():
        dk_t[...] = (dk_acc[...] * scale).T.astype(jnp.bfloat16)
        dv_t[...] = dv_acc[...].T.astype(jnp.bfloat16)


def attention_grads(bounds, probs, ctx_t, out_t, inv_sum, queries, k_t, values):
    total = queries.shape[0]
    n = total // QBLK
    per = QBLK // ctx_t.shape[2]
    lanes = lambda rows: pl.BlockSpec((rows, QBLK), lambda i, b: (0, i))
    whole = lambda shape: pl.BlockSpec(shape, lambda i, b: (0, 0))
    return pl.pallas_call(
        grads_kernel,
        grid_spec=pltpu.PrefetchScalarGridSpec(
            num_scalar_prefetch=1,
            grid=(n,),
            in_specs=[
                pl.BlockSpec((None, total, QBLK), lambda i, b: (i, 0, 0)),
                pl.BlockSpec((per, HD, ctx_t.shape[2]), lambda i, b: (i, 0, 0)),
                lanes(HD),
                lanes(1),
                pl.BlockSpec((QBLK, HD), lambda i, b: (i, 0)),
                whole((HD, total)),
                whole((total, HD)),
            ],
            out_specs=[lanes(HD), whole((HD, total)), whole((HD, total))],
            scratch_shapes=[pltpu.VMEM((total, HD), jnp.float32)] * 2,
        ),
        out_shape=[jax.ShapeDtypeStruct((HD, total), jnp.bfloat16)] * 3,
        compiler_params=pltpu.CompilerParams(vmem_limit_bytes=20 << 20),
        cost_estimate=pl.CostEstimate(
            flops=2 * total * total * HD * 4,
            transcendentals=0,
            bytes_accessed=total * total * 2,
        ),
        name="attention_grads",
    )(bounds, probs, ctx_t, out_t, inv_sum, queries, k_t, values)


def pick_kernel(core, low, high, attn, out):
    width = low.shape[1]
    out[:, :width] = low[...]
    out[:, width : 2 * width] = high[...]
    out[:, 2 * width :] = attn[...]


def picked_weights(core, w_in, w_attn_out):
    rows, width = w_attn_out.shape
    half = pl.BlockSpec((rows, width // 2), lambda i, c: (0, c[0]))
    return pl.pallas_call(
        pick_kernel,
        grid_spec=pltpu.PrefetchScalarGridSpec(
            num_scalar_prefetch=1,
            grid=(1,),
            in_specs=[
                half,
                pl.BlockSpec((rows, width // 2), lambda i, c: (0, c[0] + 2)),
                pl.BlockSpec((rows, width), lambda i, c: (0, 0)),
            ],
            out_specs=pl.BlockSpec((rows, 2 * width), lambda i, c: (0, 0)),
        ),
        out_shape=jax.ShapeDtypeStruct((rows, 2 * width), w_in.dtype),
        cost_estimate=pl.CostEstimate(
            flops=0, transcendentals=0, bytes_accessed=8 * rows * width
        ),
        name="picked_weights",
    )(core.reshape(1).astype(jnp.int32), w_in, w_in, w_attn_out)


def norm_kernel(own, other, piece, mine, theirs):
    over = (((1,), (1,)), ((), ()))
    weights = piece[...]
    mine[...] = lax.dot_general(own[...], weights, over, preferred_element_type=jnp.float32)
    part = lax.dot_general(other[...], weights, over, preferred_element_type=jnp.float32)
    theirs[...] = part.astype(jnp.bfloat16)


def norm_products(own, other, gathered):
    rows, width = own.shape
    out = gathered.shape[0]
    gathered = pltpu.with_memory_space_constraint(gathered, pltpu.HBM)
    whole = pl.BlockSpec((rows, width), lambda i: (0, 0))
    lanes = pl.BlockSpec((rows, BLK), lambda i: (0, i))
    return pl.pallas_call(
        norm_kernel,
        grid=(out // BLK,),
        in_specs=[whole, whole, pl.BlockSpec((BLK, width), lambda i: (i, 0))],
        out_specs=[lanes, lanes],
        out_shape=[
            jax.ShapeDtypeStruct((rows, out), jnp.float32),
            jax.ShapeDtypeStruct((rows, out), jnp.bfloat16),
        ],
        compiler_params=pltpu.CompilerParams(vmem_limit_bytes=10 << 20),
        cost_estimate=pl.CostEstimate(
            flops=4 * rows * width * out, transcendentals=0, bytes_accessed=2 * width * out
        ),
        name="norm_products",
    )(own, other, gathered)


def local(
    grad_out,
    saved_input,
    pre_glu,
    queries,
    keys,
    values,
    frame_counts,
    norm_gain,
    kernel,
    w_in,
    w_conv_out,
    w_attn_out,
):
    t_dev, width = grad_out.shape
    n_seq = lax.axis_size(TIME)
    total = t_dev * n_seq
    core = lax.axis_index("core")
    ends = frame_ends(frame_counts[0])

    gathered = lax.all_gather(picked_weights(core, w_in, w_attn_out), GROUPS, axis=0, tiled=True)

    positions = jnp.arange(total, dtype=jnp.int32)
    passed = positions[None, :] >= ends[:, None]
    lo = jnp.max(jnp.where(passed, ends[:, None], 0), axis=0, keepdims=True)
    hi = jnp.min(jnp.where(passed, total, ends[:, None]), axis=0, keepdims=True)
    bounds = jnp.stack([lo[0, ::QBLK] // BLK, (hi[0, QBLK - 1 :: QBLK] + BLK - 1) // BLK])

    conv_half, _ = halves(w_conv_out, core)
    by_y = spread(conv_half, ("far", "y"))
    ext_pos = lax.axis_index(TIME) * t_dev + jnp.arange(-HALO, t_dev + HALO, dtype=jnp.int32)
    seg_ext = jnp.broadcast_to(segments_of(ends, ext_pos)[:, None], (t_dev + 2 * HALO, LANES))
    gate_sig = jax.nn.sigmoid(pre_glu[:, width:].astype(jnp.float32))
    glu_out = (pre_glu[:, :width].astype(jnp.float32) * gate_sig).astype(jnp.bfloat16)
    glu_ext = padded(glu_out, HALO)
    by_y, lo = lax.optimization_barrier((by_y, lo))
    by_xy = spread(by_y, "x")
    probs, out_t, inv_sum = attention_probs(bounds, queries.T, keys, values.T, lo, hi)
    factor = conv_factor(seg_ext, glu_ext, kernel)
    by_xy, probs, factor = lax.optimization_barrier((by_xy, probs, factor))
    w_conv_half = by_xy.transpose(1, 0, 2, 3).reshape(width, width // 2)

    conv_out_grad = pair_product(*halves(grad_out, core), w_conv_half)
    conv_grad = (conv_out_grad * factor).astype(jnp.bfloat16)
    grad_ext = padded(conv_grad, HALO)
    low_grad, high_grad, rows = conv_grads(seg_ext, grad_ext, glu_ext, pre_glu, kernel)
    low_own, low_away = halves(low_grad, core)
    high_own, high_away = halves(high_grad, core)

    rows = rows.reshape(2, n_seq // 2, (KW + 1) // n_seq, width).transpose(1, 0, 2, 3)
    rows = rows.reshape(n_seq, (KW + 1) // n_seq, width)
    rows = jnp.sum(lax.all_to_all(rows, TIME, split_axis=0, concat_axis=0), axis=0)

    gathered, rows = lax.optimization_barrier((gathered, rows))
    w_attn = gathered[:, width:]
    away = swap(jnp.concatenate([low_away, high_away], axis=1))
    norm_grad, back = norm_products(
        jnp.concatenate([low_own, high_own], axis=1), away, gathered
    )
    norm_grad = norm_grad + swap(back).astype(jnp.float32)
    inputs = saved_input.astype(jnp.float32)
    centred = inputs - jnp.mean(inputs, axis=1, keepdims=True)
    inv_std = 1.0 / jnp.sqrt(jnp.mean(centred * centred, axis=1, keepdims=True) + 1e-05)
    normed = centred * inv_std
    scaled_grad = norm_grad * norm_gain
    input_grad = inv_std * (
        scaled_grad
        - jnp.mean(scaled_grad, axis=1, keepdims=True)
        - normed * jnp.mean(scaled_grad * normed, axis=1, keepdims=True)
    )
    resid_grad = (grad_out.astype(jnp.float32) + input_grad).astype(jnp.bfloat16)
    ctx_t = jnp.einsum("rc,tc->rt", w_attn, resid_grad, preferred_element_type=jnp.float32)
    ctx_t = ctx_t.astype(jnp.bfloat16).reshape(n_seq, HD, t_dev)
    gain = jnp.sum(norm_grad * normed, axis=0, keepdims=True)
    ctx_t, gain = lax.optimization_barrier((ctx_t, gain))
    ctx_t = lax.all_to_all(ctx_t, TIME, split_axis=0, concat_axis=0)
    sums = jnp.concatenate([rows, gain], axis=0)
    for bit in (1, 2):
        sums = sums + lax.ppermute(sums, "y", [(i, i ^ bit) for i in range(lax.axis_size("y"))])
    ctx_t, sums = lax.optimization_barrier((ctx_t, sums))
    probs = pltpu.with_memory_space_constraint(probs, pltpu.HBM)
    stacked = spread(sums, ("far", "x"))
    grads = attention_grads(bounds, probs, ctx_t, out_t, inv_sum, queries, keys.T, values)
    query_grad, key_grad, value_grad = [array.T for array in grads]
    stacked, query_grad = lax.optimization_barrier((stacked, query_grad))
    stacked = spread(jnp.sum(stacked, axis=0), "z")
    stacked = lax.all_gather(stacked, "core", axis=0)
    kernel_grad = stacked[:, :, :-1].reshape(KW + 1, width)[:KW]
    gain_grad = jnp.sum(stacked[:, :, -1], axis=(0, 1))
    return (resid_grad, query_grad, key_grad, value_grad, kernel_grad, gain_grad)


def solution(mesh):
    dp, seq = mesh.devices.shape
    shape = (2, dp // 8, 4, seq // 2, 2)
    fine = Mesh(mesh.devices.reshape(shape), GROUPS + TIME)
    frames = P(GROUPS + TIME, None)
    heads = P(GROUPS, TIME)
    group = P(GROUPS, None)
    in_specs = (
        frames,
        frames,
        frames,
        heads,
        heads,
        heads,
        group,
        P(),
        P(),
        group,
        group,
        group,
    )
    out_specs = (frames, heads, heads, heads, P(), P())
    return jax.shard_map(local, mesh=fine, in_specs=in_specs, out_specs=out_specs, check_vma=False)
```

```python
import math

import jax
import jax.numpy as jnp
from jax import lax
from jax.experimental import pallas as pl
from jax.experimental.pallas import tpu as pltpu
from jax.sharding import Mesh
from jax.sharding import PartitionSpec as P

HD = 80
KW = 31
QBLK = 512
BLK = 256
HALO = 16
LANES = 128
TIME = ("z", "core")
GROUPS = ("far", "y", "x")


def frame_ends(frame_lens):
    n = frame_lens.shape[0]
    upto = jnp.arange(n)[:, None] >= jnp.arange(n)[None, :]
    return jnp.sum(jnp.where(upto, frame_lens[None, :], 0), axis=1).astype(jnp.int32)


def segments_of(ends, positions):
    counted = jnp.sum((positions[:, None] >= ends[None, :]).astype(jnp.int32), axis=1)
    return jnp.where(positions < 0, jnp.int32(-1), counted)


def padded(block, width):
    count = lax.axis_size(TIME)
    forward = [(i, i + 1) for i in range(count - 1)]
    backward = [(target, source) for source, target in forward]
    low = lax.ppermute(block[block.shape[0] - width :], TIME, forward)
    high = lax.ppermute(block[:width], TIME, backward)
    return jnp.concatenate([low, block, high], axis=0)


def spread(piece, axis):
    count = lax.axis_size(axis)
    copies = jnp.broadcast_to(piece[None], (count,) + piece.shape)
    return lax.all_to_all(copies, axis, split_axis=0, concat_axis=0)


def row_product(active, piece):
    return jnp.einsum("tc,rc->tr", active, piece, preferred_element_type=jnp.float32)


def halves(array, core):
    width = array.shape[1] // 2
    own = lax.dynamic_slice_in_dim(array, core * width, width, 1)
    away = lax.dynamic_slice_in_dim(array, (1 - core) * width, width, 1)
    return own, away


def swap(array):
    return lax.ppermute(array, "core", [(0, 1), (1, 0)])


def pair_product(own, away, piece):
    other = swap(away)
    back = swap(row_product(other, piece).astype(jnp.bfloat16))
    return row_product(own, piece) + back.astype(jnp.float32)


def fill_matches(seg, matches):
    rows = matches.shape[1]
    own = seg[pl.ds(HALO, rows), :]
    for tap in range(KW):
        there = seg[pl.ds(tap + HALO - KW // 2, rows), :]
        matches[tap] = jnp.where(there == own, 1.0, 0.0)


def conv_kernel(seg, glu, taps, factor, matches, wide):
    rows = factor.shape[0]

    @pl.when(pl.program_id(0) == 0)
    def _():
        fill_matches(seg, matches)

    wide[...] = glu[...].astype(jnp.float32)
    out = jnp.zeros(factor.shape, jnp.float32)
    for tap in range(KW):
        seen = wide[pl.ds(tap + HALO - KW // 2, rows), :] * matches[tap]
        out = out + taps[pl.ds(tap, 1), :] * seen
    sig = 1.0 / (1.0 + jnp.exp(-out))
    factor[...] = sig * (1.0 + out * (1.0 - sig))


def conv_factor(seg, glu_ext, taps):
    ext, width = glu_ext.shape
    rows = ext - 2 * HALO
    lanes = lambda count: pl.BlockSpec((count, LANES), lambda i: (0, i))
    return pl.pallas_call(
        conv_kernel,
        grid=(width // LANES,),
        in_specs=[pl.BlockSpec((ext, LANES), lambda i: (0, 0)), lanes(ext), lanes(KW)],
        out_specs=lanes(rows),
        out_shape=jax.ShapeDtypeStruct((rows, width), jnp.float32),
        scratch_shapes=[
            pltpu.VMEM((KW, rows, LANES), jnp.float32),
            pltpu.VMEM((ext, LANES), jnp.float32),
        ],
        compiler_params=pltpu.CompilerParams(vmem_limit_bytes=10 << 20),
        cost_estimate=pl.CostEstimate(
            flops=4 * KW * rows * width, transcendentals=rows * width, bytes_accessed=8 * rows * width
        ),
        name="conv_factor",
    )(seg, glu_ext, taps)


def conv_grads_kernel(
    seg, grad, glu, first_ref, gate_ref, taps, low, high, tap_grad, matches, wide_grad, wide_glu
):
    rows = low.shape[0]

    @pl.when(pl.program_id(0) == 0)
    def _():
        fill_matches(seg, matches)

    wide_grad[...] = grad[...].astype(jnp.float32)
    wide_glu[...] = glu[...].astype(jnp.float32)
    own = wide_grad[pl.ds(HALO, rows), :]
    glu_grad = jnp.zeros(low.shape, jnp.float32)
    for tap in range(KW):
        at = pl.ds(tap + HALO - KW // 2, rows)
        match = matches[tap]
        glu_grad = glu_grad + taps[pl.ds(KW - 1 - tap, 1), :] * (wide_grad[at, :] * match)
        tap_grad[pl.ds(tap, 1), :] = jnp.sum(own * (wide_glu[at, :] * match), axis=0, keepdims=True)
    tap_grad[pl.ds(KW, 1), :] = jnp.zeros((1, LANES), jnp.float32)
    first = first_ref[...].astype(jnp.float32)
    sig = 1.0 / (1.0 + jnp.exp(-gate_ref[...].astype(jnp.float32)))
    part = glu_grad * sig
    low[...] = part.astype(jnp.bfloat16)
    high[...] = (part * first * (1.0 - sig)).astype(jnp.bfloat16)


def conv_grads(seg, grad_ext, glu_ext, pre_glu, taps):
    ext, width = glu_ext.shape
    rows = ext - 2 * HALO
    n = width // LANES
    lanes = lambda count: pl.BlockSpec((count, LANES), lambda i: (0, i))
    return pl.pallas_call(
        conv_grads_kernel,
        grid=(n,),
        in_specs=[
            pl.BlockSpec((ext, LANES), lambda i: (0, 0)),
            lanes(ext),
            lanes(ext),
            lanes(rows),
            pl.BlockSpec((rows, LANES), lambda i: (0, i + n)),
            lanes(KW),
        ],
        out_specs=[lanes(rows), lanes(rows), lanes(KW + 1)],
        out_shape=[
            jax.ShapeDtypeStruct((rows, width), jnp.bfloat16),
            jax.ShapeDtypeStruct((rows, width), jnp.bfloat16),
            jax.ShapeDtypeStruct((KW + 1, width), jnp.float32),
        ],
        scratch_shapes=[
            pltpu.VMEM((KW, rows, LANES), jnp.float32),
            pltpu.VMEM((ext, LANES), jnp.float32),
            pltpu.VMEM((ext, LANES), jnp.float32),
        ],
        compiler_params=pltpu.CompilerParams(vmem_limit_bytes=10 << 20),
        cost_estimate=pl.CostEstimate(
            flops=8 * KW * rows * width, transcendentals=rows * width, bytes_accessed=16 * rows * width
        ),
        name="conv_grads",
    )(seg, grad_ext, glu_ext, pre_glu, pre_glu, taps)


def over_keys(first, last, step, carry):
    pairs = (last - first) // 2

    def pair(i, carry):
        return step(pl.multiple_of((first + 2 * i) * BLK, BLK), 2 * BLK, carry)

    def single(i, carry):
        return step(pl.multiple_of(i * BLK, BLK), BLK, carry)

    carry = lax.fori_loop(0, pairs, pair, carry)
    return lax.fori_loop(first + 2 * pairs, last, single, carry)


def probs_kernel(bounds, q_t, k, v_t, lo, hi, probs, out_t, inv_sum, scores):
    factor = math.log2(math.e) / math.sqrt(HD)
    block = pl.program_id(0)
    first = bounds[0, block]
    last = bounds[1, block]
    query = q_t[...]
    start = lo[...]
    end = hi[...]
    width = query.shape[1]

    def score(at, size, peak):
        rows = lax.broadcasted_iota(jnp.int32, (size, width), 0)
        s = jnp.dot(k[pl.ds(at, size), :], query, preferred_element_type=jnp.float32)
        valid = (rows >= start - at) & (rows < end - at)
        s = jnp.where(valid, s, -1e30)
        scores[pl.ds(at, size), :] = s
        return jnp.maximum(peak, jnp.max(s.reshape(size // 8, 8, width), axis=0))

    peak = over_keys(first, last, score, jnp.full((8, width), -1e30, jnp.float32))
    peak = jnp.max(peak, axis=0, keepdims=True)

    def expo(at, size, carry):
        total, acc = carry
        e = jnp.exp2((scores[pl.ds(at, size), :] - peak) * factor)
        low = e.astype(jnp.bfloat16)
        probs[pl.ds(at, size), :] = low
        acc = acc + jnp.dot(v_t[:, pl.ds(at, size)], low, preferred_element_type=jnp.float32)
        return total + jnp.sum(e.reshape(size // 8, 8, width), axis=0), acc

    total, acc = over_keys(
        first,
        last,
        expo,
        (jnp.zeros((8, width), jnp.float32), jnp.zeros((HD, width), jnp.float32)),
    )
    inv = 1.0 / jnp.sum(total, axis=0, keepdims=True)
    inv_sum[...] = inv
    out_t[...] = acc * inv


def attention_probs(bounds, q_t, keys, v_t, lo, hi):
    total = keys.shape[0]
    n = total // QBLK
    lanes = lambda rows: pl.BlockSpec((rows, QBLK), lambda i, b: (0, i))
    whole = lambda shape: pl.BlockSpec(shape, lambda i, b: (0, 0))
    return pl.pallas_call(
        probs_kernel,
        grid_spec=pltpu.PrefetchScalarGridSpec(
            num_scalar_prefetch=1,
            grid=(n,),
            in_specs=[
                lanes(HD),
                whole((total, HD)),
                whole((HD, total)),
                lanes(1),
                lanes(1),
            ],
            out_specs=[
                pl.BlockSpec((None, total, QBLK), lambda i, b: (i, 0, 0)),
                lanes(HD),
                lanes(1),
            ],
            scratch_shapes=[pltpu.VMEM((total, QBLK), jnp.float32)],
        ),
        out_shape=[
            pltpu.HBM((n, total, QBLK), jnp.bfloat16),
            jax.ShapeDtypeStruct((HD, total), jnp.float32),
            jax.ShapeDtypeStruct((1, total), jnp.float32),
        ],
        compiler_params=pltpu.CompilerParams(vmem_limit_bytes=20 << 20),
        cost_estimate=pl.CostEstimate(
            flops=2 * total * total * HD * 2,
            transcendentals=total * total // 2,
            bytes_accessed=total * total * 2,
        ),
        name="attention_probs",
    )(bounds, q_t, keys, v_t, lo, hi)


def grads_kernel(bounds, probs, ctx_t, out_t, inv_sum, q, k_t, v, dq_t, dk_t, dv_t, dk_acc, dv_acc):
    scale = 1.0 / math.sqrt(HD)
    block = pl.program_id(0)
    first = bounds[0, block]
    last = bounds[1, block]

    @pl.when(block == 0)
    def _():
        dk_acc[...] = jnp.zeros_like(dk_acc)
        dv_acc[...] = jnp.zeros_like(dv_acc)

    pieces = [ctx_t[i].astype(jnp.float32) for i in range(ctx_t.shape[0])]
    grad_t = jnp.concatenate(pieces, axis=1) * inv_sum[...]
    grad_low_t = grad_t.astype(jnp.bfloat16)
    grad_low = grad_t.T.astype(jnp.bfloat16)
    delta = jnp.sum(grad_low_t.astype(jnp.float32) * out_t[...], axis=0, keepdims=True)
    query = q[...]

    def step(at, size, acc):
        e = probs[pl.ds(at, size), :]
        prob_grad = jnp.dot(v[pl.ds(at, size), :], grad_low_t, preferred_element_type=jnp.float32)
        ds = (e.astype(jnp.float32) * (prob_grad - delta)).astype(jnp.bfloat16)
        dv_acc[pl.ds(at, size), :] += jnp.dot(e, grad_low, preferred_element_type=jnp.float32)
        dk_acc[pl.ds(at, size), :] += jnp.dot(ds, query, preferred_element_type=jnp.float32)
        return acc + jnp.dot(k_t[:, pl.ds(at, size)], ds, preferred_element_type=jnp.float32)

    acc = over_keys(first, last, step, jnp.zeros((HD, query.shape[0]), jnp.float32))
    dq_t[...] = (acc * scale).astype(jnp.bfloat16)

    @pl.when(block == pl.num_programs(0) - 1)
    def _():
        dk_t[...] = (dk_acc[...] * scale).T.astype(jnp.bfloat16)
        dv_t[...] = dv_acc[...].T.astype(jnp.bfloat16)


def attention_grads(bounds, probs, ctx_t, out_t, inv_sum, queries, k_t, values):
    total = queries.shape[0]
    n = total // QBLK
    per = QBLK // ctx_t.shape[2]
    lanes = lambda rows: pl.BlockSpec((rows, QBLK), lambda i, b: (0, i))
    whole = lambda shape: pl.BlockSpec(shape, lambda i, b: (0, 0))
    return pl.pallas_call(
        grads_kernel,
        grid_spec=pltpu.PrefetchScalarGridSpec(
            num_scalar_prefetch=1,
            grid=(n,),
            in_specs=[
                pl.BlockSpec((None, total, QBLK), lambda i, b: (i, 0, 0)),
                pl.BlockSpec((per, HD, ctx_t.shape[2]), lambda i, b: (i, 0, 0)),
                lanes(HD),
                lanes(1),
                pl.BlockSpec((QBLK, HD), lambda i, b: (i, 0)),
                whole((HD, total)),
                whole((total, HD)),
            ],
            out_specs=[lanes(HD), whole((HD, total)), whole((HD, total))],
            scratch_shapes=[pltpu.VMEM((total, HD), jnp.float32)] * 2,
        ),
        out_shape=[jax.ShapeDtypeStruct((HD, total), jnp.bfloat16)] * 3,
        compiler_params=pltpu.CompilerParams(vmem_limit_bytes=20 << 20),
        cost_estimate=pl.CostEstimate(
            flops=2 * total * total * HD * 4,
            transcendentals=0,
            bytes_accessed=total * total * 2,
        ),
        name="attention_grads",
    )(bounds, probs, ctx_t, out_t, inv_sum, queries, k_t, values)


def pick_kernel(core, low, high, attn, out):
    width = low.shape[1]
    out[:, :width] = low[...]
    out[:, width : 2 * width] = high[...]
    out[:, 2 * width :] = attn[...]


def picked_weights(core, w_in, w_attn_out):
    rows, width = w_attn_out.shape
    half = pl.BlockSpec((rows, width // 2), lambda i, c: (0, c[0]))
    return pl.pallas_call(
        pick_kernel,
        grid_spec=pltpu.PrefetchScalarGridSpec(
            num_scalar_prefetch=1,
            grid=(1,),
            in_specs=[
                half,
                pl.BlockSpec((rows, width // 2), lambda i, c: (0, c[0] + 2)),
                pl.BlockSpec((rows, width), lambda i, c: (0, 0)),
            ],
            out_specs=pl.BlockSpec((rows, 2 * width), lambda i, c: (0, 0)),
        ),
        out_shape=jax.ShapeDtypeStruct((rows, 2 * width), w_in.dtype),
        cost_estimate=pl.CostEstimate(
            flops=0, transcendentals=0, bytes_accessed=8 * rows * width
        ),
        name="picked_weights",
    )(core.reshape(1).astype(jnp.int32), w_in, w_in, w_attn_out)


def norm_kernel(own, other, piece, mine, theirs, both):
    rows = own.shape[0]

    @pl.when(pl.program_id(0) == 0)
    def _():
        both[:rows, :] = own[...]
        both[rows:, :] = other[...]

    product = lax.dot_general(
        both[...], piece[...], (((1,), (1,)), ((), ())), preferred_element_type=jnp.float32
    )
    mine[...] = product[:rows]
    theirs[...] = product[rows:].astype(jnp.bfloat16)


def norm_products(own, other, gathered):
    rows, width = own.shape
    out = gathered.shape[0]
    step = out // 2
    gathered = pltpu.with_memory_space_constraint(gathered, pltpu.HBM)
    whole = pl.BlockSpec((rows, width), lambda i: (0, 0))
    lanes = pl.BlockSpec((rows, step), lambda i: (0, i))
    return pl.pallas_call(
        norm_kernel,
        grid=(out // step,),
        in_specs=[whole, whole, pl.BlockSpec((step, width), lambda i: (i, 0))],
        out_specs=[lanes, lanes],
        out_shape=[
            jax.ShapeDtypeStruct((rows, out), jnp.float32),
            jax.ShapeDtypeStruct((rows, out), jnp.bfloat16),
        ],
        scratch_shapes=[pltpu.VMEM((2 * rows, width), jnp.bfloat16)],
        compiler_params=pltpu.CompilerParams(vmem_limit_bytes=10 << 20),
        cost_estimate=pl.CostEstimate(
            flops=4 * rows * width * out, transcendentals=0, bytes_accessed=2 * width * out
        ),
        name="norm_products",
    )(own, other, gathered)


def local(
    grad_out,
    saved_input,
    pre_glu,
    queries,
    keys,
    values,
    frame_counts,
    norm_gain,
    kernel,
    w_in,
    w_conv_out,
    w_attn_out,
):
    t_dev, width = grad_out.shape
    n_seq = lax.axis_size(TIME)
    total = t_dev * n_seq
    core = lax.axis_index("core")
    ends = frame_ends(frame_counts[0])

    gathered = lax.all_gather(picked_weights(core, w_in, w_attn_out), GROUPS, axis=0, tiled=True)

    positions = jnp.arange(total, dtype=jnp.int32)
    passed = positions[None, :] >= ends[:, None]
    lo = jnp.max(jnp.where(passed, ends[:, None], 0), axis=0, keepdims=True)
    hi = jnp.min(jnp.where(passed, total, ends[:, None]), axis=0, keepdims=True)
    bounds = jnp.stack([lo[0, ::QBLK] // BLK, (hi[0, QBLK - 1 :: QBLK] + BLK - 1) // BLK])

    conv_half, _ = halves(w_conv_out, core)
    by_y = spread(conv_half, ("far", "y"))
    ext_pos = lax.axis_index(TIME) * t_dev + jnp.arange(-HALO, t_dev + HALO, dtype=jnp.int32)
    seg_ext = jnp.broadcast_to(segments_of(ends, ext_pos)[:, None], (t_dev + 2 * HALO, LANES))
    gate_sig = jax.nn.sigmoid(pre_glu[:, width:].astype(jnp.float32))
    glu_out = (pre_glu[:, :width].astype(jnp.float32) * gate_sig).astype(jnp.bfloat16)
    glu_ext = padded(glu_out, HALO)
    by_y, lo = lax.optimization_barrier((by_y, lo))
    by_xy = spread(by_y, "x")
    probs, out_t, inv_sum = attention_probs(bounds, queries.T, keys, values.T, lo, hi)
    factor = conv_factor(seg_ext, glu_ext, kernel)
    by_xy, probs, factor = lax.optimization_barrier((by_xy, probs, factor))
    w_conv_half = by_xy.transpose(1, 0, 2, 3).reshape(width, width // 2)

    conv_out_grad = pair_product(*halves(grad_out, core), w_conv_half)
    conv_grad = (conv_out_grad * factor).astype(jnp.bfloat16)
    grad_ext = padded(conv_grad, HALO)
    low_grad, high_grad, rows = conv_grads(seg_ext, grad_ext, glu_ext, pre_glu, kernel)
    low_own, low_away = halves(low_grad, core)
    high_own, high_away = halves(high_grad, core)

    rows = rows.reshape(2, n_seq // 2, (KW + 1) // n_seq, width).transpose(1, 0, 2, 3)
    rows = rows.reshape(n_seq, (KW + 1) // n_seq, width)
    rows = jnp.sum(lax.all_to_all(rows, TIME, split_axis=0, concat_axis=0), axis=0)

    gathered, rows = lax.optimization_barrier((gathered, rows))
    w_attn = gathered[:, width:]
    away = swap(jnp.concatenate([low_away, high_away], axis=1))
    norm_grad, back = norm_products(
        jnp.concatenate([low_own, high_own], axis=1), away, gathered
    )
    norm_grad = norm_grad + swap(back).astype(jnp.float32)
    inputs = saved_input.astype(jnp.float32)
    centred = inputs - jnp.mean(inputs, axis=1, keepdims=True)
    inv_std = 1.0 / jnp.sqrt(jnp.mean(centred * centred, axis=1, keepdims=True) + 1e-05)
    normed = centred * inv_std
    scaled_grad = norm_grad * norm_gain
    input_grad = inv_std * (
        scaled_grad
        - jnp.mean(scaled_grad, axis=1, keepdims=True)
        - normed * jnp.mean(scaled_grad * normed, axis=1, keepdims=True)
    )
    resid_grad = (grad_out.astype(jnp.float32) + input_grad).astype(jnp.bfloat16)
    ctx_t = jnp.einsum("rc,tc->rt", w_attn, resid_grad, preferred_element_type=jnp.float32)
    ctx_t = ctx_t.astype(jnp.bfloat16).reshape(n_seq, HD, t_dev)
    gain = jnp.sum(norm_grad * normed, axis=0, keepdims=True)
    ctx_t, gain = lax.optimization_barrier((ctx_t, gain))
    ctx_t = lax.all_to_all(ctx_t, TIME, split_axis=0, concat_axis=0)
    sums = jnp.concatenate([rows, gain], axis=0)
    for bit in (1, 2):
        sums = sums + lax.ppermute(sums, "y", [(i, i ^ bit) for i in range(lax.axis_size("y"))])
    ctx_t, sums = lax.optimization_barrier((ctx_t, sums))
    probs = pltpu.with_memory_space_constraint(probs, pltpu.HBM)
    stacked = spread(sums, ("far", "x"))
    grads = attention_grads(bounds, probs, ctx_t, out_t, inv_sum, queries, keys.T, values)
    query_grad, key_grad, value_grad = [array.T for array in grads]
    stacked, query_grad = lax.optimization_barrier((stacked, query_grad))
    stacked = spread(jnp.sum(stacked, axis=0), "z")
    stacked = lax.all_gather(stacked, "core", axis=0)
    kernel_grad = stacked[:, :, :-1].reshape(KW + 1, width)[:KW]
    gain_grad = jnp.sum(stacked[:, :, -1], axis=(0, 1))
    return (resid_grad, query_grad, key_grad, value_grad, kernel_grad, gain_grad)


def solution(mesh):
    dp, seq = mesh.devices.shape
    shape = (2, dp // 8, 4, seq // 2, 2)
    fine = Mesh(mesh.devices.reshape(shape), GROUPS + TIME)
    frames = P(GROUPS + TIME, None)
    heads = P(GROUPS, TIME)
    group = P(GROUPS, None)
    in_specs = (
        frames,
        frames,
        frames,
        heads,
        heads,
        heads,
        group,
        P(),
        P(),
        group,
        group,
        group,
    )
    out_specs = (frames, heads, heads, heads, P(), P())
    return jax.shard_map(local, mesh=fine, in_specs=in_specs, out_specs=out_specs, check_vma=False)
```
